32 devices in a mesh: groups: 2 (over y), tm: 4 (over z), chan: 2 (over x), sub: 2 (over core).
Axes of the slice: x: 2, y: 2, z: 4, core: 2. Of those that a mesh axis runs over, the one named last changes fastest.
Arguments:
- traces: bfloat16 [512, 8192], P(('chan', 'sub'), ('groups', 'tm')), parts along dimension 1, may hold values from -60 to 60
- templates: bfloat16 [32, 512, 256], P('tm', ('chan', 'sub')), may hold values from -6 to 6
- channel_mask: int32 [32, 512], P('tm', ('chan', 'sub')), may hold values from 0 to 1
Outputs:
- scores: float32 [32, 8192], P(('chan', 'sub'), ('groups', 'tm')), parts along dimension 1
The draws below stay inside these ranges and needn't reach their ends.
There are 2 independent parts, one for each index of `groups`. The reference program is written for one: setup_inputs(seed, part) draws one part's arguments, and reference() takes and returns one part's arrays. A program takes and returns all parts, laid end to end along the dimension named above; an argument that names none is the same for every part. Nothing has to cross between parts.
All inputs are finite; a program needn't handle non-finite values.
Results may differ from the reference program's by a relative error of at most 0.0003.
Values may be sent and summed in bfloat16 or wider, within the bound.
No kernel may reach another device: no remote copies, remote signals or barrier semaphores. Data moves between devices by JAX's collectives and lax.ppermute only.
A program may use at most 64 MiB of HBM per device.

```python
import jax
import jax.numpy as jnp
from jax import lax

S = 256
TEMPLATES = 32
CHANNELS = 512
TIME = 4096


def draw_traces(key, part):
    scale_key, envelope_key, noise_key = jax.random.split(key, 3)
    chan_scale = jnp.exp(jax.random.uniform(scale_key, (CHANNELS, 1), jnp.float32, 0.0, 2.3))
    envelope = jnp.exp(jax.random.uniform(envelope_key, (1, TIME // 64), jnp.float32, -0.7, 0.7))
    envelope = jnp.repeat(envelope, 64, axis=1)
    noise = jax.random.normal(noise_key, (CHANNELS, TIME), jnp.float32)
    values = jnp.clip(noise * chan_scale * envelope, -60.0, 60.0)
    return values.astype(jnp.bfloat16)


def mask_pattern(key):
    mask_key, drop_key = jax.random.split(jax.random.fold_in(key, 7))
    used = jax.random.randint(mask_key, (TEMPLATES, CHANNELS), 0, 2, jnp.int32)
    dropped = jax.random.randint(drop_key, (TEMPLATES, CHANNELS), 0, 16, jnp.int32)
    silent = used * (dropped == 0).astype(jnp.int32)
    return (used, silent)


def draw_channel_mask(key, part):
    used, silent = mask_pattern(key)
    return used


def draw_templates(key, part):
    used, silent = mask_pattern(key)
    wave_key = jax.random.fold_in(key, 11)
    values = jnp.clip(jax.random.normal(wave_key, (TEMPLATES, CHANNELS, S), jnp.float32), -6.0, 6.0)
    keep = (1 - silent).astype(jnp.float32)[:, :, None]
    return (values * keep).astype(jnp.bfloat16)


def setup_inputs(seed: int = 0, part: int = 0) -> dict:
    arg_keys = jax.random.split(jax.random.key(seed), 4)
    part_splits = jax.random.split(jax.random.fold_in(arg_keys[3], part), 4)
    return {
        "traces": draw_traces(jax.random.fold_in(jax.random.fold_in(arg_keys[3], part), 71), part),
        "templates": draw_templates(jax.random.fold_in(arg_keys[3], 71), part),
        "channel_mask": draw_channel_mask(jax.random.fold_in(arg_keys[3], 71), part),
    }


EPSILON = 1e-06

def reference(traces, templates, channel_mask):
    signal = traces.astype(jnp.float32)
    wrapped = jnp.concatenate([signal, signal[:, :S]], 1)
    squares = wrapped * wrapped
    masked = templates * channel_mask.astype(jnp.bfloat16)[:, :, None]
    weights = masked.astype(jnp.float32)

    def advance(state_tuple, offset):
        correlation, chan_energy = state_tuple
        window = lax.dynamic_slice_in_dim(wrapped, offset, TIME, 1)
        lag_weights = lax.dynamic_index_in_dim(weights, offset, 2, keepdims=False)
        correlation = correlation + jnp.dot(lag_weights, window, precision=lax.Precision.HIGHEST, preferred_element_type=jnp.float32)
        chan_energy = chan_energy + lax.dynamic_slice_in_dim(squares, offset, TIME, 1)
        return ((correlation, chan_energy), None)
    initial = (jnp.zeros((TEMPLATES, TIME), jnp.float32), jnp.zeros((CHANNELS, TIME), jnp.float32))
    (correlation, chan_energy), _ = lax.scan(advance, initial, jnp.arange(S, dtype=jnp.int32))
    active = channel_mask.astype(jnp.float32)
    template_energy = lax.optimization_barrier(jnp.sum(weights * weights, axis=(1, 2)))
    active_count = lax.optimization_barrier(jnp.sum(active, axis=1))
    energy = jnp.dot(active, chan_energy, precision=lax.Precision.HIGHEST, preferred_element_type=jnp.float32)
    factor = jnp.sqrt(S * active_count)[:, None]
    return correlation * factor / jnp.sqrt(energy * template_energy[:, None] + EPSILON)
```

```python
import functools
import math

import jax
import jax.numpy as jnp
from jax import lax
from jax.experimental import pallas as pl
from jax.experimental.pallas import tpu as pltpu
from jax.sharding import PartitionSpec as P

EPSILON = 1e-06
LANE = 128
FRAMES = 4
STEP = LANE // FRAMES
IN_VMEM = pl.BlockSpec(memory_space=pltpu.VMEM)


def shifted(x, axis, by):
    count = lax.axis_size(axis)
    return lax.ppermute(x, axis, [(i, (i + by) % count) for i in range(count)])


def arrange(masked, span):
    rows, chans, _ = masked.shape
    split = masked.reshape(rows, chans, span // LANE, FRAMES, STEP)
    return split.transpose(4, 0, 2, 3, 1).reshape(STEP * rows, span * chans // STEP)


def correlate(weights, signal, frames, partial, rows, width):
    chans = signal.shape[0]
    depth = FRAMES * chans
    blocks = weights.shape[1] // depth
    extent = width + LANE
    reach = extent + (blocks - 1) * LANE
    signal = jnp.concatenate(
        [signal, jnp.zeros((chans, reach + LANE - signal.shape[1]), signal.dtype)], 1
    )
    for frame in range(FRAMES):
        frames[frame * chans : (frame + 1) * chans, :] = signal[:, frame * STEP : frame * STEP + reach]
    total = None
    for block in range(blocks):
        term = jnp.dot(
            weights[:, block * depth : (block + 1) * depth],
            frames[:, block * LANE : block * LANE + extent],
            preferred_element_type=jnp.float32,
        )
        total = term if total is None else total + term
    partial[...] = total
    result = partial[0:rows, 0:width]
    for lag in range(1, STEP):
        result = result + partial[lag * rows : (lag + 1) * rows, lag : lag + width]
    return result


def channel_squares(active, signal):
    wide = signal.astype(jnp.float32)
    squares = wide * wide
    high = squares.astype(jnp.bfloat16)
    low = (squares - high.astype(jnp.float32)).astype(jnp.bfloat16)
    return jnp.dot(
        jnp.concatenate([active, active], 1),
        jnp.concatenate([high, low], 0),
        preferred_element_type=jnp.float32,
    )


def pair_kernel(span, weights, active, first, second, head, corr, squares, frames, partial):
    rows, width = corr.shape
    signal = jnp.concatenate([first[...], second[...], head[:, :span]], 1)
    corr[...] = correlate(weights, signal, frames, partial, rows, width)
    squares[...] = channel_squares(active[...], signal[:, :width])


def pair_scratch(chans, rows, width, span):
    extent = width + LANE
    return [
        pltpu.VMEM((FRAMES * chans, extent + span - LANE), jnp.bfloat16),
        pltpu.VMEM((STEP * rows, extent), jnp.float32),
    ]


def pair_call(weights, active, first, second, head, span):
    rows, chans = active.shape
    width = 2 * first.shape[1]
    shape = jax.ShapeDtypeStruct((rows, width), jnp.float32)
    flops = 2 * weights.shape[0] * weights.shape[1] * (width + LANE)
    return pl.pallas_call(
        functools.partial(pair_kernel, span),
        out_shape=(shape, shape),
        in_specs=[IN_VMEM] * 5,
        out_specs=(IN_VMEM, IN_VMEM),
        scratch_shapes=pair_scratch(chans, rows, width, span),
        cost_estimate=pl.CostEstimate(flops=flops, bytes_accessed=1 << 20, transcendentals=0),
        compiler_params=pltpu.CompilerParams(vmem_limit_bytes=32 << 20),
    )(weights, active, first, second, head)


def window_sums(values, span):
    reach = 1
    while reach < span:
        values = values + jnp.concatenate([values[:, reach:], values[:, :reach]], 1)
        reach *= 2
    return values


def pack_kernel(span, ways, tile, pairs, place, stats, *refs):
    corrs, squares = refs[:pairs], refs[pairs : 2 * pairs]
    outs, corr_all, energy_all = refs[2 * pairs : -2], refs[-2], refs[-1]
    rows, total = corr_all.shape
    corr = jnp.concatenate([ref[...] for ref in corrs], 1)
    corr_all[...] = jnp.concatenate([corr[:, tile:], corr[:, :tile]], 1)
    energy = window_sums(jnp.concatenate([ref[...] for ref in squares], 1), span)
    energy_all[...] = jnp.concatenate([energy[:, tile:], energy[:, :tile]], 1)
    part = total // ways
    for shift in range(ways):
        start = pl.multiple_of(lax.rem(place[0] + shift, ways) * part, LANE)
        outs[shift][0:rows, 0:part] = corr_all[:, pl.ds(start, part)]
        outs[shift][rows : 2 * rows, 0:part] = energy_all[:, pl.ds(start, part)]
        outs[shift][:, part:] = stats[...]


def pack_call(place, stats, corrs, squares, span, ways):
    rows, width = corrs[0].shape
    pairs = len(corrs)
    total = pairs * width
    shape = jax.ShapeDtypeStruct((2 * rows, total // ways + LANE), jnp.float32)
    return pl.pallas_call(
        functools.partial(pack_kernel, span, ways, width // 2, pairs),
        out_shape=(shape,) * ways,
        in_specs=[pl.BlockSpec(memory_space=pltpu.SMEM)] + [IN_VMEM] * (1 + 2 * pairs),
        out_specs=(IN_VMEM,) * ways,
        scratch_shapes=[pltpu.VMEM((rows, total), jnp.float32)] * 2,
        compiler_params=pltpu.CompilerParams(vmem_limit_bytes=16 << 20),
    )(place, stats, *corrs, *squares)


def split_kernel(ways, count, place, *refs):
    ins, outs, held = refs[:count], refs[count:-1], refs[-1]
    total = ins[0][...]
    for ref in ins[1:]:
        total = total + ref[...]
    held[...] = total
    part = (held.shape[1] - LANE) // ways
    for shift in range(ways):
        start = pl.multiple_of(lax.rem(place[0] + shift, ways) * part, LANE)
        outs[shift][:, 0:part] = held[:, pl.ds(start, part)]
        outs[shift][:, part:] = held[:, part * ways :]


def split_call(place, parts, ways):
    rows, width = parts[0].shape
    shape = jax.ShapeDtypeStruct((rows, (width - LANE) // ways + LANE), jnp.float32)
    return pl.pallas_call(
        functools.partial(split_kernel, ways, len(parts)),
        out_shape=(shape,) * ways,
        in_specs=[pl.BlockSpec(memory_space=pltpu.SMEM)] + [IN_VMEM] * len(parts),
        out_specs=(IN_VMEM,) * ways,
        scratch_shapes=[pltpu.VMEM((rows, width), jnp.float32)],
        compiler_params=pltpu.CompilerParams(vmem_limit_bytes=16 << 20),
    )(place, *parts)


def score_kernel(span, count, *refs):
    ins, out = refs[:count], refs[count]
    total = ins[0][...]
    for ref in ins[1:]:
        total = total + ref[...]
    rows, width = out.shape
    template_energy = total[0:rows, width : width + 1]
    active_count = total[rows:, width : width + 1]
    factor = jnp.sqrt(span * active_count)
    energy = total[rows:, 0:width]
    out[...] = total[0:rows, 0:width] * factor / jnp.sqrt(energy * template_energy + EPSILON)


def score_call(parts, span):
    rows, width = parts[0].shape
    return pl.pallas_call(
        functools.partial(score_kernel, span, len(parts)),
        out_shape=jax.ShapeDtypeStruct((rows // 2, width - LANE), jnp.float32),
        in_specs=[IN_VMEM] * len(parts),
        out_specs=IN_VMEM,
        compiler_params=pltpu.CompilerParams(vmem_limit_bytes=16 << 20),
    )(*parts)


def exchange(parts, axis):
    return [parts[0]] + [shifted(part, axis, shift) for shift, part in enumerate(parts) if shift]


def on_device(traces, templates, channel_mask):
    tile = traces.shape[1]
    rows, _, span = templates.shape
    circle = lax.axis_size("tm")
    chan_ways, sub_ways = lax.axis_size("chan"), lax.axis_size("sub")
    arrived = {0: traces}
    for hop in range(1, circle // 2 + 1):
        for near in dict.fromkeys((hop, circle - hop)):
            arrived[near] = shifted(traces, "tm", -near)
    active = channel_mask.astype(jnp.bfloat16)
    masked = templates * active[:, :, None]
    weights = arrange(masked, span)
    wide = masked.astype(jnp.float32)
    template_energy = jnp.sum(wide * wide, axis=(1, 2))
    active_count = jnp.sum(channel_mask, axis=1).astype(jnp.float32)
    stats = jnp.concatenate([template_energy, active_count])
    stats = jnp.broadcast_to(stats[:, None], (2 * rows, LANE))

    corrs, squares = [], []
    for pair in range(circle // 2):
        first = (2 * pair - 1) % circle
        corr, square = pair_call(
            weights,
            active,
            arrived[first],
            arrived[2 * pair],
            arrived[(2 * pair + 1) % circle],
            span,
        )
        corrs.append(corr)
        squares.append(square)
    sub_place = lax.axis_index("sub").astype(jnp.int32)[None]
    chan_place = lax.axis_index("chan").astype(jnp.int32)[None]
    parts = exchange(pack_call(sub_place, stats, corrs, squares, span, sub_ways), "sub")
    parts = exchange(split_call(chan_place, parts, chan_ways), "chan")
    scores = score_call(parts, span)

    held = circle // (chan_ways * sub_ways)
    received = []
    for piece in range(held):
        pairs = []
        for place in range(circle):
            for chan in range(chan_ways):
                for sub in range(sub_ways):
                    start = (sub * chan_ways + chan) * held
                    time_tile = (place + start + piece) % circle
                    source = (place * chan_ways + chan) * sub_ways + sub
                    target = time_tile * chan_ways * sub_ways + place // held
                    pairs.append((source, target))
        block = scores[:, piece * tile : (piece + 1) * tile]
        received.append(lax.ppermute(block, ("tm", "chan", "sub"), pairs))
    if held == 1:
        return received[0]
    order = (lax.axis_index("tm") - jnp.arange(held)) % held
    return jnp.stack(received)[order].reshape(held * rows, tile)


def solution(mesh):
    placed = (
        P(("chan", "sub"), ("groups", "tm")),
        P("tm", ("chan", "sub"), None),
        P("tm", ("chan", "sub")),
    )
    return jax.shard_map(
        on_device,
        mesh=mesh,
        in_specs=placed,
        out_specs=P(("chan", "sub"), ("groups", "tm")),
        check_vma=False,
    )
```

```python
import functools

import jax
import jax.numpy as jnp
from jax import lax
from jax.experimental import pallas as pl
from jax.experimental.pallas import tpu as pltpu
from jax.sharding import PartitionSpec as P

EPSILON = 1e-06
LANE = 128
FRAMES = 4
STEP = LANE // FRAMES
IN_VMEM = pl.BlockSpec(memory_space=pltpu.VMEM)


def shifted(x, axis, by):
    count = lax.axis_size(axis)
    return lax.ppermute(x, axis, [(i, (i + by) % count) for i in range(count)])


def arrange(masked, span):
    rows, chans, _ = masked.shape
    split = masked.reshape(rows, chans, span // LANE, FRAMES, STEP)
    return split.transpose(4, 0, 2, 3, 1).reshape(STEP * rows, span * chans // STEP)


def correlate(weights, signal, frames, partial, rows, width):
    chans = signal.shape[0]
    depth = FRAMES * chans
    blocks = weights.shape[1] // depth
    extent = width + LANE
    reach = extent + (blocks - 1) * LANE
    signal = jnp.concatenate(
        [signal, jnp.zeros((chans, reach + LANE - signal.shape[1]), signal.dtype)], 1
    )
    for frame in range(FRAMES):
        frames[frame * chans : (frame + 1) * chans, :] = signal[:, frame * STEP : frame * STEP + reach]
    total = None
    for block in range(blocks):
        term = jnp.dot(
            weights[:, block * depth : (block + 1) * depth],
            frames[:, block * LANE : block * LANE + extent],
            preferred_element_type=jnp.float32,
        )
        total = term if total is None else total + term
    partial[...] = total
    result = partial[0:rows, 0:width]
    for lag in range(1, STEP):
        result = result + partial[lag * rows : (lag + 1) * rows, lag : lag + width]
    return result


def channel_squares(active, signal):
    wide = signal.astype(jnp.float32)
    squares = wide * wide
    high = squares.astype(jnp.bfloat16)
    low = (squares - high.astype(jnp.float32)).astype(jnp.bfloat16)
    return jnp.dot(
        jnp.concatenate([active, active], 1),
        jnp.concatenate([high, low], 0),
        preferred_element_type=jnp.float32,
    )


def pair_kernel(span, weights, active, first, second, head, corr, squares, frames, partial):
    rows, width = corr.shape
    signal = jnp.concatenate([first[...], second[...], head[:, :span]], 1)
    corr[...] = correlate(weights, signal, frames, partial, rows, width)
    squares[...] = channel_squares(active[...], signal[:, :width])


def pair_scratch(chans, rows, width, span):
    extent = width + LANE
    return [
        pltpu.VMEM((FRAMES * chans, extent + span - LANE), jnp.bfloat16),
        pltpu.VMEM((STEP * rows, extent), jnp.float32),
    ]


def pair_call(weights, active, first, second, head, span):
    rows, chans = active.shape
    width = 2 * first.shape[1]
    shape = jax.ShapeDtypeStruct((rows, width), jnp.float32)
    flops = 2 * weights.shape[0] * weights.shape[1] * (width + LANE)
    return pl.pallas_call(
        functools.partial(pair_kernel, span),
        out_shape=(shape, shape),
        in_specs=[IN_VMEM] * 5,
        out_specs=(IN_VMEM, IN_VMEM),
        scratch_shapes=pair_scratch(chans, rows, width, span),
        cost_estimate=pl.CostEstimate(flops=flops, bytes_accessed=1 << 20, transcendentals=0),
        compiler_params=pltpu.CompilerParams(vmem_limit_bytes=32 << 20),
    )(weights, active, first, second, head)


def early_kernel(span, odd, weights, active, own, near, far, corr, squares, edges, frames, partial):
    rows, width = corr.shape
    swap = odd[0] == 1
    first = jnp.where(swap, far[...], own[...])
    third = jnp.where(swap, own[...], far[...])
    signal = jnp.concatenate([first, near[...], third], 1)
    corr[...] = correlate(weights, signal, frames, partial, rows, width)
    squares[...] = channel_squares(active[...], signal)
    edges[:, :span] = signal[:, width:]
    edges[:, span:] = first[:, :span]


def early_call(odd, weights, active, own, near, far, span):
    rows, chans = active.shape
    total = 3 * own.shape[1]
    width = total - span
    flops = 2 * weights.shape[0] * weights.shape[1] * total
    return pl.pallas_call(
        functools.partial(early_kernel, span),
        out_shape=(
            jax.ShapeDtypeStruct((rows, width), jnp.float32),
            jax.ShapeDtypeStruct((rows, total), jnp.float32),
            jax.ShapeDtypeStruct((chans, 2 * span), own.dtype),
        ),
        in_specs=[pl.BlockSpec(memory_space=pltpu.SMEM)] + [IN_VMEM] * 5,
        out_specs=(IN_VMEM,) * 3,
        scratch_shapes=pair_scratch(chans, rows, width, span),
        cost_estimate=pl.CostEstimate(flops=flops, bytes_accessed=1 << 20, transcendentals=0),
        compiler_params=pltpu.CompilerParams(vmem_limit_bytes=32 << 20),
    )(odd, weights, active, own, near, far)


def late_kernel(span, ways, place, weights, active, stats, last, edges, corr, squares, *refs):
    outs, (corr_all, energy_all, frames, partial) = refs[:ways], refs[ways:]
    rows, total = corr_all.shape
    early = corr.shape[1]
    signal = jnp.concatenate([edges[:, :span], last[...], edges[:, span:]], 1)
    corr_all[:, :early] = corr[...]
    corr_all[:, early:] = correlate(weights, signal, frames, partial, rows, total - early)
    energy_all[...] = window_sums(
        jnp.concatenate([squares[...], channel_squares(active[...], last[...])], 1), span
    )
    share(place, corr_all, energy_all, stats, outs)


def late_call(place, weights, active, stats, last, edges, corr, squares, span, ways):
    rows, early = corr.shape
    chans, tile = last.shape
    total = early + span + tile
    shape = jax.ShapeDtypeStruct((2 * rows, total // ways + LANE), jnp.float32)
    flops = 2 * weights.shape[0] * weights.shape[1] * (tile + span)
    return pl.pallas_call(
        functools.partial(late_kernel, span, ways),
        out_shape=(shape,) * ways,
        in_specs=[pl.BlockSpec(memory_space=pltpu.SMEM)] + [IN_VMEM] * 7,
        out_specs=(IN_VMEM,) * ways,
        scratch_shapes=[pltpu.VMEM((rows, total), jnp.float32)] * 2
        + pair_scratch(chans, rows, total - early, span),
        cost_estimate=pl.CostEstimate(flops=flops, bytes_accessed=1 << 20, transcendentals=0),
        compiler_params=pltpu.CompilerParams(vmem_limit_bytes=32 << 20),
    )(place, weights, active, stats, last, edges, corr, squares)


def share(place, corr_all, energy_all, stats, outs):
    rows, total = corr_all.shape
    ways = len(outs)
    part = total // ways
    for shift in range(ways):
        start = pl.multiple_of(lax.rem(place[0] + shift, ways) * part, LANE)
        outs[shift][0:rows, 0:part] = corr_all[:, pl.ds(start, part)]
        outs[shift][rows : 2 * rows, 0:part] = energy_all[:, pl.ds(start, part)]
        outs[shift][:, part:] = stats[...]


def window_sums(values, span):
    reach = 1
    while reach < span:
        values = values + jnp.concatenate([values[:, reach:], values[:, :reach]], 1)
        reach *= 2
    return values


def pack_kernel(span, ways, tile, pairs, place, stats, *refs):
    corrs, squares = refs[:pairs], refs[pairs : 2 * pairs]
    outs, corr_all, energy_all = refs[2 * pairs : -2], refs[-2], refs[-1]
    rows, total = corr_all.shape
    corr = jnp.concatenate([ref[...] for ref in corrs], 1)
    corr_all[...] = jnp.concatenate([corr[:, tile:], corr[:, :tile]], 1)
    energy = window_sums(jnp.concatenate([ref[...] for ref in squares], 1), span)
    energy_all[...] = jnp.concatenate([energy[:, tile:], energy[:, :tile]], 1)
    share(place, corr_all, energy_all, stats, outs)


def pack_call(place, stats, corrs, squares, span, ways):
    rows, width = corrs[0].shape
    pairs = len(corrs)
    total = pairs * width
    shape = jax.ShapeDtypeStruct((2 * rows, total // ways + LANE), jnp.float32)
    return pl.pallas_call(
        functools.partial(pack_kernel, span, ways, width // 2, pairs),
        out_shape=(shape,) * ways,
        in_specs=[pl.BlockSpec(memory_space=pltpu.SMEM)] + [IN_VMEM] * (1 + 2 * pairs),
        out_specs=(IN_VMEM,) * ways,
        scratch_shapes=[pltpu.VMEM((rows, total), jnp.float32)] * 2,
        compiler_params=pltpu.CompilerParams(vmem_limit_bytes=16 << 20),
    )(place, stats, *corrs, *squares)


def split_kernel(ways, count, place, *refs):
    ins, outs, held = refs[:count], refs[count:-1], refs[-1]
    total = ins[0][...]
    for ref in ins[1:]:
        total = total + ref[...]
    held[...] = total
    part = (held.shape[1] - LANE) // ways
    for shift in range(ways):
        start = pl.multiple_of(lax.rem(place[0] + shift, ways) * part, LANE)
        outs[shift][:, 0:part] = held[:, pl.ds(start, part)]
        outs[shift][:, part:] = held[:, part * ways :]


def split_call(place, parts, ways):
    rows, width = parts[0].shape
    shape = jax.ShapeDtypeStruct((rows, (width - LANE) // ways + LANE), jnp.float32)
    return pl.pallas_call(
        functools.partial(split_kernel, ways, len(parts)),
        out_shape=(shape,) * ways,
        in_specs=[pl.BlockSpec(memory_space=pltpu.SMEM)] + [IN_VMEM] * len(parts),
        out_specs=(IN_VMEM,) * ways,
        scratch_shapes=[pltpu.VMEM((rows, width), jnp.float32)],
        compiler_params=pltpu.CompilerParams(vmem_limit_bytes=16 << 20),
    )(place, *parts)


def score_kernel(span, count, *refs):
    ins, out = refs[:count], refs[count]
    total = ins[0][...]
    for ref in ins[1:]:
        total = total + ref[...]
    rows, width = out.shape
    template_energy = total[0:rows, width : width + 1]
    active_count = total[rows:, width : width + 1]
    factor = jnp.sqrt(span * active_count)
    energy = total[rows:, 0:width]
    out[...] = total[0:rows, 0:width] * factor / jnp.sqrt(energy * template_energy + EPSILON)


def score_call(parts, span):
    rows, width = parts[0].shape
    return pl.pallas_call(
        functools.partial(score_kernel, span, len(parts)),
        out_shape=jax.ShapeDtypeStruct((rows // 2, width - LANE), jnp.float32),
        in_specs=[IN_VMEM] * len(parts),
        out_specs=IN_VMEM,
        compiler_params=pltpu.CompilerParams(vmem_limit_bytes=16 << 20),
    )(*parts)


def exchange(parts, axis):
    return [parts[0]] + [shifted(part, axis, shift) for shift, part in enumerate(parts) if shift]


def paired(x, axis, bit):
    return lax.ppermute(x, axis, [(i, i ^ bit) for i in range(lax.axis_size(axis))])


def relayed_sums(traces, weights, active, stats, sub_place, span, ways):
    far = paired(traces, "tm", 2)
    near = paired(traces, "tm", 1)
    last = paired(far, "tm", 1)
    odd = (lax.axis_index("tm") % 2).astype(jnp.int32)[None]
    corr, squares, edges = early_call(odd, weights, active, traces, near, far, span)
    return late_call(sub_place, weights, active, stats, last, edges, corr, squares, span, ways)


def gathered_sums(traces, weights, active, stats, sub_place, span, ways):
    circle = lax.axis_size("tm")
    arrived = {0: traces}
    for hop in range(1, circle // 2 + 1):
        for near in dict.fromkeys((hop, circle - hop)):
            arrived[near] = shifted(traces, "tm", -near)
    corrs, squares = [], []
    for pair in range(circle // 2):
        first, second = arrived[(2 * pair - 1) % circle], arrived[2 * pair]
        head = arrived[(2 * pair + 1) % circle]
        corr, square = pair_call(weights, active, first, second, head, span)
        corrs.append(corr)
        squares.append(square)
    return pack_call(sub_place, stats, corrs, squares, span, ways)


def on_device(traces, templates, channel_mask):
    tile = traces.shape[1]
    rows, _, span = templates.shape
    circle = lax.axis_size("tm")
    chan_ways, sub_ways = lax.axis_size("chan"), lax.axis_size("sub")
    active = channel_mask.astype(jnp.bfloat16)
    masked = templates * active[:, :, None]
    weights = arrange(masked, span)
    wide = masked.astype(jnp.float32)
    template_energy = jnp.sum(wide * wide, axis=(1, 2))
    active_count = jnp.sum(channel_mask, axis=1).astype(jnp.float32)
    stats = jnp.concatenate([template_energy, active_count])
    stats = jnp.broadcast_to(stats[:, None], (2 * rows, LANE))
    sub_place = lax.axis_index("sub").astype(jnp.int32)[None]
    chan_place = lax.axis_index("chan").astype(jnp.int32)[None]
    relayed = circle == 4
    sums = relayed_sums if relayed else gathered_sums
    parts = sums(traces, weights, active, stats, sub_place, span, sub_ways)
    parts = exchange(parts, "sub")
    parts = exchange(split_call(chan_place, parts, chan_ways), "chan")
    scores = score_call(parts, span)

    held = circle // (chan_ways * sub_ways)
    received = []
    for piece in range(held):
        pairs = []
        for place in range(circle):
            for chan in range(chan_ways):
                for sub in range(sub_ways):
                    start = (sub * chan_ways + chan) * held + piece
                    time_tile = (start - place if relayed else start + place) % circle
                    source = (place * chan_ways + chan) * sub_ways + sub
                    target = time_tile * chan_ways * sub_ways + place // held
                    pairs.append((source, target))
        block = scores[:, piece * tile : (piece + 1) * tile]
        received.append(lax.ppermute(block, ("tm", "chan", "sub"), pairs))
    if held == 1:
        return received[0]
    order = (lax.axis_index("tm") - jnp.arange(held)) % held
    return jnp.stack(received)[order].reshape(held * rows, tile)


def solution(mesh):
    placed = (
        P(("chan", "sub"), ("groups", "tm")),
        P("tm", ("chan", "sub"), None),
        P("tm", ("chan", "sub")),
    )
    return jax.shard_map(
        on_device,
        mesh=mesh,
        in_specs=placed,
        out_specs=P(("chan", "sub"), ("groups", "tm")),
        check_vma=False,
    )
```

```python
import functools

import jax
import jax.numpy as jnp
from jax import lax
from jax.experimental import pallas as pl
from jax.experimental.pallas import tpu as pltpu
from jax.sharding import PartitionSpec as P

EPSILON = 1e-06
LANE = 128
FRAMES = 4
STEP = LANE // FRAMES
IN_VMEM = pl.BlockSpec(memory_space=pltpu.VMEM)


def shifted(x, axis, by):
    count = lax.axis_size(axis)
    return lax.ppermute(x, axis, [(i, (i + by) % count) for i in range(count)])


def arrange(masked, span):
    rows, chans, _ = masked.shape
    split = masked.reshape(rows, chans, span // LANE, FRAMES, STEP)
    return split.transpose(4, 0, 2, 3, 1).reshape(STEP * rows, span * chans // STEP)


def correlate(weights, signal, frames, partial, rows, width):
    chans = signal.shape[0]
    depth = FRAMES * chans
    blocks = weights.shape[1] // depth
    extent = width + LANE
    reach = extent + (blocks - 1) * LANE
    signal = jnp.concatenate(
        [signal, jnp.zeros((chans, reach + LANE - signal.shape[1]), signal.dtype)], 1
    )
    for frame in range(FRAMES):
        frames[frame * chans : (frame + 1) * chans, :] = signal[:, frame * STEP : frame * STEP + reach]
    total = None
    for block in range(blocks):
        term = jnp.dot(
            weights[:, block * depth : (block + 1) * depth],
            frames[:, block * LANE : block * LANE + extent],
            preferred_element_type=jnp.float32,
        )
        total = term if total is None else total + term
    partial[...] = total
    result = partial[0:rows, 0:width]
    for lag in range(1, STEP):
        result = result + partial[lag * rows : (lag + 1) * rows, lag : lag + width]
    return result


def channel_squares(active, signal):
    wide = signal.astype(jnp.float32)
    squares = wide * wide
    high = squares.astype(jnp.bfloat16)
    low = (squares - high.astype(jnp.float32)).astype(jnp.bfloat16)
    return jnp.dot(
        jnp.concatenate([active, active], 1),
        jnp.concatenate([high, low], 0),
        preferred_element_type=jnp.float32,
    )


def pair_kernel(span, weights, active, first, second, head, corr, squares, frames, partial):
    rows, width = corr.shape
    signal = jnp.concatenate([first[...], second[...], head[:, :span]], 1)
    corr[...] = correlate(weights, signal, frames, partial, rows, width)
    squares[...] = channel_squares(active[...], signal[:, :width])


def pair_scratch(chans, rows, width, span):
    extent = width + LANE
    return [
        pltpu.VMEM((FRAMES * chans, extent + span - LANE), jnp.bfloat16),
        pltpu.VMEM((STEP * rows, extent), jnp.float32),
    ]


def pair_call(weights, active, first, second, head, span):
    rows, chans = active.shape
    width = 2 * first.shape[1]
    shape = jax.ShapeDtypeStruct((rows, width), jnp.float32)
    flops = 2 * weights.shape[0] * weights.shape[1] * (width + LANE)
    return pl.pallas_call(
        functools.partial(pair_kernel, span),
        out_shape=(shape, shape),
        in_specs=[IN_VMEM] * 5,
        out_specs=(IN_VMEM, IN_VMEM),
        scratch_shapes=pair_scratch(chans, rows, width, span),
        cost_estimate=pl.CostEstimate(flops=flops, bytes_accessed=1 << 20, transcendentals=0),
        compiler_params=pltpu.CompilerParams(vmem_limit_bytes=32 << 20),
    )(weights, active, first, second, head)


def early_kernel(span, odd, stats, weights, active, own, near, far, corr, energy, wide, edges, squares, frames, partial):
    rows, width = corr.shape
    swap = odd[0] == 1
    first = jnp.where(swap, far[...], own[...])
    third = jnp.where(swap, own[...], far[...])
    signal = jnp.concatenate([first, near[...], third], 1)
    corr[...] = correlate(weights, signal, frames, partial, rows, width)
    sums = channel_squares(active[...], signal)
    energy[...] = line_sums(sums, span)[:, :width]
    edges[:, :span] = signal[:, width:]
    edges[:, span:] = first[:, :span]
    squares[:, :span] = sums[:, width:]
    squares[:, span:] = sums[:, :span]
    wide[...] = jnp.broadcast_to(stats[...], wide.shape)


def early_call(odd, stats, weights, active, own, near, far, span):
    rows, chans = active.shape
    total = 3 * own.shape[1]
    width = total - span
    flops = 2 * weights.shape[0] * weights.shape[1] * total
    return pl.pallas_call(
        functools.partial(early_kernel, span),
        out_shape=(
            jax.ShapeDtypeStruct((rows, width), jnp.float32),
            jax.ShapeDtypeStruct((rows, width), jnp.float32),
            jax.ShapeDtypeStruct((2 * rows, LANE), jnp.float32),
            jax.ShapeDtypeStruct((chans, 2 * span), own.dtype),
            jax.ShapeDtypeStruct((rows, 2 * span), jnp.float32),
        ),
        in_specs=[pl.BlockSpec(memory_space=pltpu.SMEM)] + [IN_VMEM] * 6,
        out_specs=(IN_VMEM,) * 5,
        scratch_shapes=pair_scratch(chans, rows, width, span),
        cost_estimate=pl.CostEstimate(flops=flops, bytes_accessed=1 << 20, transcendentals=0),
        compiler_params=pltpu.CompilerParams(vmem_limit_bytes=32 << 20),
    )(odd, stats, weights, active, own, near, far)


def late_kernel(span, ways, place, order, weights, active, last, corr, energy, stats, edges, squares, *refs):
    outs, (corr_all, energy_all, frames, partial) = refs[:ways], refs[ways:]
    rows, total = corr_all.shape
    early = corr.shape[1]
    signal = jnp.concatenate([edges[:, :span], last[...], edges[:, span:]], 1)
    sums = channel_squares(active[...], last[...])
    sums = jnp.concatenate([squares[:, :span], sums, squares[:, span:]], 1)
    energy_all[:, :early] = energy[...]
    energy_all[:, early:] = line_sums(sums, span)[:, : total - early]
    corr_all[:, :early] = corr[...]
    corr_all[:, early:] = correlate(weights, signal, frames, partial, rows, total - early)
    share(place, order, last.shape[1], corr_all, energy_all, stats, outs)


def late_call(place, order, weights, active, last, early, span, ways):
    rows, done = early[0].shape
    chans, tile = last.shape
    total = done + span + tile
    shape = jax.ShapeDtypeStruct((2 * rows, total // ways + LANE), jnp.float32)
    flops = 2 * weights.shape[0] * weights.shape[1] * (tile + span)
    return pl.pallas_call(
        functools.partial(late_kernel, span, ways),
        out_shape=(shape,) * ways,
        in_specs=[pl.BlockSpec(memory_space=pltpu.SMEM)] * 2 + [IN_VMEM] * 8,
        out_specs=(IN_VMEM,) * ways,
        scratch_shapes=[pltpu.VMEM((rows, total), jnp.float32)] * 2
        + pair_scratch(chans, rows, total - done, span),
        cost_estimate=pl.CostEstimate(flops=flops, bytes_accessed=1 << 20, transcendentals=0),
        compiler_params=pltpu.CompilerParams(vmem_limit_bytes=32 << 20),
    )(place, order, weights, active, last, *early)


def share(place, order, tile, corr_all, energy_all, stats, outs):
    rows, total = corr_all.shape
    ways = len(outs)
    count = total // tile // ways
    for shift in range(ways):
        group = lax.rem(place[0] + shift, ways) * count
        for item in range(count):
            start = pl.multiple_of(order[group + item] * tile, LANE)
            columns = slice(item * tile, (item + 1) * tile)
            outs[shift][0:rows, columns] = corr_all[:, pl.ds(start, tile)]
            outs[shift][rows : 2 * rows, columns] = energy_all[:, pl.ds(start, tile)]
        outs[shift][:, count * tile :] = stats[...]


def line_sums(values, span):
    reach = 1
    while reach < span:
        values = values + jnp.concatenate([values[:, reach:], values[:, :reach]], 1)
        reach *= 2
    return values


def pack_kernel(span, tile, pairs, place, order, stats, *refs):
    corrs, squares = refs[:pairs], refs[pairs : 2 * pairs]
    outs, corr_all, energy_all = refs[2 * pairs : -2], refs[-2], refs[-1]
    corr = jnp.concatenate([ref[...] for ref in corrs], 1)
    corr_all[...] = jnp.concatenate([corr[:, tile:], corr[:, :tile]], 1)
    energy = line_sums(jnp.concatenate([ref[...] for ref in squares], 1), span)
    energy_all[...] = jnp.concatenate([energy[:, tile:], energy[:, :tile]], 1)
    share(place, order, tile, corr_all, energy_all, stats, outs)


def pack_call(place, order, stats, corrs, squares, span, ways):
    rows, width = corrs[0].shape
    pairs = len(corrs)
    total = pairs * width
    shape = jax.ShapeDtypeStruct((2 * rows, total // ways + LANE), jnp.float32)
    return pl.pallas_call(
        functools.partial(pack_kernel, span, width // 2, pairs),
        out_shape=(shape,) * ways,
        in_specs=[pl.BlockSpec(memory_space=pltpu.SMEM)] * 2 + [IN_VMEM] * (1 + 2 * pairs),
        out_specs=(IN_VMEM,) * ways,
        scratch_shapes=[pltpu.VMEM((rows, total), jnp.float32)] * 2,
        compiler_params=pltpu.CompilerParams(vmem_limit_bytes=16 << 20),
    )(place, order, stats, *corrs, *squares)


def split_kernel(ways, count, place, *refs):
    ins, outs, held = refs[:count], refs[count:-1], refs[-1]
    total = ins[0][...]
    for ref in ins[1:]:
        total = total + ref[...]
    held[...] = total
    part = (held.shape[1] - LANE) // ways
    for shift in range(ways):
        start = pl.multiple_of(lax.rem(place[0] + shift, ways) * part, LANE)
        outs[shift][:, 0:part] = held[:, pl.ds(start, part)]
        outs[shift][:, part:] = held[:, part * ways :]


def split_call(place, parts, ways):
    rows, width = parts[0].shape
    shape = jax.ShapeDtypeStruct((rows, (width - LANE) // ways + LANE), jnp.float32)
    return pl.pallas_call(
        functools.partial(split_kernel, ways, len(parts)),
        out_shape=(shape,) * ways,
        in_specs=[pl.BlockSpec(memory_space=pltpu.SMEM)] + [IN_VMEM] * len(parts),
        out_specs=(IN_VMEM,) * ways,
        scratch_shapes=[pltpu.VMEM((rows, width), jnp.float32)],
        compiler_params=pltpu.CompilerParams(vmem_limit_bytes=16 << 20),
    )(place, *parts)


def score_kernel(span, count, *refs):
    ins, out = refs[:count], refs[count]
    total = ins[0][...]
    for ref in ins[1:]:
        total = total + ref[...]
    rows, width = out.shape
    template_energy = total[0:rows, width : width + 1]
    active_count = total[rows:, width : width + 1]
    factor = jnp.sqrt(span * active_count)
    energy = total[rows:, 0:width]
    out[...] = total[0:rows, 0:width] * factor / jnp.sqrt(energy * template_energy + EPSILON)


def score_call(parts, span):
    rows, width = parts[0].shape
    return pl.pallas_call(
        functools.partial(score_kernel, span, len(parts)),
        out_shape=jax.ShapeDtypeStruct((rows // 2, width - LANE), jnp.float32),
        in_specs=[IN_VMEM] * len(parts),
        out_specs=IN_VMEM,
        compiler_params=pltpu.CompilerParams(vmem_limit_bytes=16 << 20),
    )(*parts)


def exchange(parts, axis):
    return [parts[0]] + [shifted(part, axis, shift) for shift, part in enumerate(parts) if shift]


def paired(x, axis, bit):
    return lax.ppermute(x, axis, [(i, i ^ bit) for i in range(lax.axis_size(axis))])


def relayed_sums(traces, weights, active, stats, sub_place, order, span, ways):
    far = paired(traces, "tm", 2)
    near = paired(traces, "tm", 1)
    last = paired(far, "tm", 1)
    odd = (lax.axis_index("tm") % 2).astype(jnp.int32)[None]
    early = early_call(odd, stats, weights, active, traces, near, far, span)
    return late_call(sub_place, order, weights, active, last, early, span, ways)


def routes(circle, chan_ways, sub_ways):
    held = circle // (chan_ways * sub_ways)
    table = []
    for place in range(circle):
        chan, sub = divmod(place // held, sub_ways)
        slots = [(s, c, h) for s in range(sub_ways) for c in range(chan_ways) for h in range(held)]
        tiles = sorted(range(circle), key=lambda t: -abs(t - place))
        ranked = sorted(range(circle), key=lambda k: (slots[k][1] != chan, slots[k][0] != sub))
        row = [0] * circle
        for slot, time_tile in zip(ranked, tiles):
            row[slot] = time_tile
        table.append(row)
    return table


def gathered_sums(traces, weights, active, stats, sub_place, order, span, ways):
    circle = lax.axis_size("tm")
    arrived = {0: traces}
    for hop in range(1, circle // 2 + 1):
        for near in dict.fromkeys((hop, circle - hop)):
            arrived[near] = shifted(traces, "tm", -near)
    corrs, squares = [], []
    for pair in range(circle // 2):
        first, second = arrived[(2 * pair - 1) % circle], arrived[2 * pair]
        head = arrived[(2 * pair + 1) % circle]
        corr, square = pair_call(weights, active, first, second, head, span)
        corrs.append(corr)
        squares.append(square)
    stats = jnp.broadcast_to(stats, (stats.shape[0], LANE))
    return pack_call(sub_place, order, stats, corrs, squares, span, ways)


def on_device(traces, templates, channel_mask):
    tile = traces.shape[1]
    rows, _, span = templates.shape
    circle = lax.axis_size("tm")
    chan_ways, sub_ways = lax.axis_size("chan"), lax.axis_size("sub")
    active = channel_mask.astype(jnp.bfloat16)
    masked = templates * active[:, :, None]
    weights = arrange(masked, span)
    wide = masked.astype(jnp.float32)
    template_energy = jnp.sum(wide * wide, axis=(1, 2))
    active_count = jnp.sum(channel_mask, axis=1).astype(jnp.float32)
    stats = jnp.concatenate([template_energy, active_count])[:, None]
    sub_place = lax.axis_index("sub").astype(jnp.int32)[None]
    chan_place = lax.axis_index("chan").astype(jnp.int32)[None]

    ways = chan_ways * sub_ways
    held = circle // ways
    relayed = circle == ways == 4
    if relayed:
        table = routes(circle, chan_ways, sub_ways)
        order = (jnp.array(table, jnp.int32)[lax.axis_index("tm")] + lax.axis_index("tm")) % circle
    else:
        table = [[(slot + place) % circle for slot in range(circle)] for place in range(circle)]
        order = jnp.arange(circle, dtype=jnp.int32)
    sums = relayed_sums if relayed else gathered_sums
    parts = sums(traces, weights, active, stats, sub_place, order.astype(jnp.int32), span, sub_ways)
    parts = exchange(parts, "sub")
    parts = exchange(split_call(chan_place, parts, chan_ways), "chan")
    scores = score_call(parts, span)

    received = []
    for piece in range(held):
        pairs = []
        for place in range(circle):
            for chan in range(chan_ways):
                for sub in range(sub_ways):
                    source = (place * chan_ways + chan) * sub_ways + sub
                    slot = (sub * chan_ways + chan) * held + piece
                    pairs.append((source, table[place][slot] * ways + place // held))
        block = scores[:, piece * tile : (piece + 1) * tile]
        received.append(lax.ppermute(block, ("tm", "chan", "sub"), pairs))
    if held == 1:
        return received[0]
    turn = (lax.axis_index("tm") - jnp.arange(held)) % held
    return jnp.stack(received)[turn].reshape(held * rows, tile)


def solution(mesh):
    placed = (
        P(("chan", "sub"), ("groups", "tm")),
        P("tm", ("chan", "sub"), None),
        P("tm", ("chan", "sub")),
    )
    return jax.shard_map(
        on_device,
        mesh=mesh,
        in_specs=placed,
        out_specs=P(("chan", "sub"), ("groups", "tm")),
        check_vma=False,
    )
```

```python
import functools

import jax
import jax.numpy as jnp
from jax import lax
from jax.experimental import pallas as pl
from jax.experimental.pallas import tpu as pltpu
from jax.sharding import PartitionSpec as P


EPSILON = 1e-06
LANE = 128
FRAMES = 4
STEP = LANE // FRAMES
IN_VMEM = pl.BlockSpec(memory_space=pltpu.VMEM)


def shifted(x, axis, by):
    count = lax.axis_size(axis)
    return lax.ppermute(x, axis, [(i, (i + by) % count) for i in range(count)])


def arrange(masked, span):
    rows, chans, _ = masked.shape
    split = masked.reshape(rows, chans, span // LANE, FRAMES, STEP)
    return split.transpose(4, 0, 2, 3, 1).reshape(STEP * rows, span * chans // STEP)


def correlate(weights, signal, frames, partial, rows, width):
    chans = signal.shape[0]
    depth = FRAMES * chans
    blocks = weights.shape[1] // depth
    extent = width + LANE
    reach = extent + (blocks - 1) * LANE
    signal = jnp.concatenate(
        [signal, jnp.zeros((chans, reach + LANE - signal.shape[1]), signal.dtype)], 1
    )
    for frame in range(FRAMES):
        frames[frame * chans : (frame + 1) * chans, :] = signal[:, frame * STEP : frame * STEP + reach]
    total = None
    for block in range(blocks):
        term = jnp.dot(
            weights[:, block * depth : (block + 1) * depth],
            frames[:, block * LANE : block * LANE + extent],
            preferred_element_type=jnp.float32,
        )
        total = term if total is None else total + term
    partial[...] = total
    result = partial[0:rows, 0:width]
    for lag in range(1, STEP):
        result = result + partial[lag * rows : (lag + 1) * rows, lag : lag + width]
    return result


def channel_squares(active, signal):
    wide = signal.astype(jnp.float32)
    squares = wide * wide
    high = squares.astype(jnp.bfloat16)
    low = (squares - high.astype(jnp.float32)).astype(jnp.bfloat16)
    return jnp.dot(
        jnp.concatenate([active, active], 1),
        jnp.concatenate([high, low], 0),
        preferred_element_type=jnp.float32,
    )


def pair_kernel(span, weights, active, first, second, head, corr, squares, frames, partial):
    rows, width = corr.shape
    signal = jnp.concatenate([first[...], second[...], head[:, :span]], 1)
    corr[...] = correlate(weights, signal, frames, partial, rows, width)
    squares[...] = channel_squares(active[...], signal[:, :width])


def pair_scratch(chans, rows, width, span):
    extent = width + LANE
    return [
        pltpu.VMEM((FRAMES * chans, extent + span - LANE), jnp.bfloat16),
        pltpu.VMEM((STEP * rows, extent), jnp.float32),
    ]


def pair_call(weights, active, first, second, head, span):
    rows, chans = active.shape
    width = 2 * first.shape[1]
    shape = jax.ShapeDtypeStruct((rows, width), jnp.float32)
    flops = 2 * weights.shape[0] * weights.shape[1] * (width + LANE)
    return pl.pallas_call(
        functools.partial(pair_kernel, span),
        out_shape=(shape, shape),
        in_specs=[IN_VMEM] * 5,
        out_specs=(IN_VMEM, IN_VMEM),
        scratch_shapes=pair_scratch(chans, rows, width, span),
        cost_estimate=pl.CostEstimate(flops=flops, bytes_accessed=1 << 20, transcendentals=0),
        compiler_params=pltpu.CompilerParams(vmem_limit_bytes=32 << 20),
    )(weights, active, first, second, head)


def early_kernel(span, odd, stats, weights, active, own, near, *refs):
    fars, (corr, energy, wide, edges, squares, frames, partial) = refs[:-7], refs[-7:]
    rows, width = corr.shape
    swap = odd[0] == 1
    far = jnp.concatenate([ref[...] for ref in fars], 1)
    first = jnp.where(swap, far, own[...])
    third = jnp.where(swap, own[...], far)
    signal = jnp.concatenate([first, near[...], third], 1)
    corr[...] = correlate(weights, signal, frames, partial, rows, width)
    sums = channel_squares(active[...], signal)
    energy[...] = line_sums(sums, span)[:, :width]
    edges[:, :span] = signal[:, width:]
    edges[:, span:] = first[:, :span]
    squares[:, :span] = sums[:, width:]
    squares[:, span:] = sums[:, :span]
    wide[...] = jnp.broadcast_to(stats[...], wide.shape)


def early_call(odd, stats, weights, active, own, near, fars, span):
    rows, chans = active.shape
    total = 3 * own.shape[1]
    width = total - span
    flops = 2 * weights.shape[0] * weights.shape[1] * total
    return pl.pallas_call(
        functools.partial(early_kernel, span),
        out_shape=(
            jax.ShapeDtypeStruct((rows, width), jnp.float32),
            jax.ShapeDtypeStruct((rows, width), jnp.float32),
            jax.ShapeDtypeStruct((2 * rows, LANE), jnp.float32),
            jax.ShapeDtypeStruct((chans, 2 * span), own.dtype),
            jax.ShapeDtypeStruct((rows, 2 * span), jnp.float32),
        ),
        in_specs=[pl.BlockSpec(memory_space=pltpu.SMEM)] + [IN_VMEM] * (5 + len(fars)),
        out_specs=(IN_VMEM,) * 5,
        scratch_shapes=pair_scratch(chans, rows, width, span),
        cost_estimate=pl.CostEstimate(flops=flops, bytes_accessed=1 << 20, transcendentals=0),
        compiler_params=pltpu.CompilerParams(vmem_limit_bytes=32 << 20),
    )(odd, stats, weights, active, own, near, *fars)


def middle_kernel(span, weights, active, part, edges, squares, corr, energy, tail, frames, partial):
    rows, width = corr.shape
    signal = jnp.concatenate([edges[:, :span], part[...]], 1)
    sums = channel_squares(active[...], part[...])
    tail[...] = sums[:, width - span :]
    sums = jnp.concatenate([squares[:, :span], sums], 1)
    energy[...] = line_sums(sums, span)[:, :width]
    corr[...] = correlate(weights, signal, frames, partial, rows, width)


def middle_call(weights, active, part, edges, squares, span):
    rows, chans = active.shape
    width = part.shape[1]
    flops = 2 * weights.shape[0] * weights.shape[1] * width
    shape = jax.ShapeDtypeStruct((rows, width), jnp.float32)
    return pl.pallas_call(
        functools.partial(middle_kernel, span),
        out_shape=(shape, shape, jax.ShapeDtypeStruct((rows, span), jnp.float32)),
        in_specs=[IN_VMEM] * 5,
        out_specs=(IN_VMEM,) * 3,
        scratch_shapes=pair_scratch(chans, rows, width, span),
        cost_estimate=pl.CostEstimate(flops=flops, bytes_accessed=1 << 20, transcendentals=0),
        compiler_params=pltpu.CompilerParams(vmem_limit_bytes=32 << 20),
    )(weights, active, part, edges, squares)


def late_kernel(span, ways, place, order, weights, active, before, part, corr, energy, stats, edges, squares, middle_corr, middle_energy, tail, *refs):
    outs, (corr_all, energy_all, frames, partial) = refs[:ways], refs[ways:]
    rows, total = corr_all.shape
    early, done = corr.shape[1], corr.shape[1] + middle_corr.shape[1]
    signal = jnp.concatenate([before[:, before.shape[1] - span :], part[...], edges[:, span:]], 1)
    sums = channel_squares(active[...], part[...])
    sums = jnp.concatenate([tail[...], sums, squares[:, span:]], 1)
    energy_all[:, :early] = energy[...]
    energy_all[:, early:done] = middle_energy[...]
    energy_all[:, done:] = line_sums(sums, span)[:, : total - done]
    corr_all[:, :early] = corr[...]
    corr_all[:, early:done] = middle_corr[...]
    corr_all[:, done:] = correlate(weights, signal, frames, partial, rows, total - done)
    share(place, order, total // order.shape[0], corr_all, energy_all, stats, outs)


def late_call(place, order, weights, active, before, part, early, middle, span, ways):
    rows = active.shape[0]
    chans, width = part.shape
    total = early[0].shape[1] + middle[0].shape[1] + span + width
    shape = jax.ShapeDtypeStruct((2 * rows, total // ways + LANE), jnp.float32)
    flops = 2 * weights.shape[0] * weights.shape[1] * (width + span)
    return pl.pallas_call(
        functools.partial(late_kernel, span, ways),
        out_shape=(shape,) * ways,
        in_specs=[pl.BlockSpec(memory_space=pltpu.SMEM)] * 2 + [IN_VMEM] * (4 + len(early) + len(middle)),
        out_specs=(IN_VMEM,) * ways,
        scratch_shapes=[pltpu.VMEM((rows, total), jnp.float32)] * 2
        + pair_scratch(chans, rows, width + span, span),
        cost_estimate=pl.CostEstimate(flops=flops, bytes_accessed=1 << 20, transcendentals=0),
        compiler_params=pltpu.CompilerParams(vmem_limit_bytes=32 << 20),
    )(place, order, weights, active, before, part, *early, *middle)


def share(place, order, tile, corr_all, energy_all, stats, outs):
    rows, total = corr_all.shape
    ways = len(outs)
    count = total // tile // ways
    for shift in range(ways):
        group = lax.rem(place[0] + shift, ways) * count
        for item in range(count):
            start = pl.multiple_of(order[group + item] * tile, LANE)
            columns = slice(item * tile, (item + 1) * tile)
            outs[shift][0:rows, columns] = corr_all[:, pl.ds(start, tile)]
            outs[shift][rows : 2 * rows, columns] = energy_all[:, pl.ds(start, tile)]
        outs[shift][:, count * tile :] = stats[...]


def line_sums(values, span):
    reach = 1
    while reach < span:
        values = values + jnp.concatenate([values[:, reach:], values[:, :reach]], 1)
        reach *= 2
    return values


def pack_kernel(span, tile, pairs, place, order, stats, *refs):
    corrs, squares = refs[:pairs], refs[pairs : 2 * pairs]
    outs, corr_all, energy_all = refs[2 * pairs : -2], refs[-2], refs[-1]
    corr = jnp.concatenate([ref[...] for ref in corrs], 1)
    corr_all[...] = jnp.concatenate([corr[:, tile:], corr[:, :tile]], 1)
    energy = line_sums(jnp.concatenate([ref[...] for ref in squares], 1), span)
    energy_all[...] = jnp.concatenate([energy[:, tile:], energy[:, :tile]], 1)
    share(place, order, tile, corr_all, energy_all, stats, outs)


def pack_call(place, order, stats, corrs, squares, span, ways):
    rows, width = corrs[0].shape
    pairs = len(corrs)
    total = pairs * width
    shape = jax.ShapeDtypeStruct((2 * rows, total // ways + LANE), jnp.float32)
    return pl.pallas_call(
        functools.partial(pack_kernel, span, width // 2, pairs),
        out_shape=(shape,) * ways,
        in_specs=[pl.BlockSpec(memory_space=pltpu.SMEM)] * 2 + [IN_VMEM] * (1 + 2 * pairs),
        out_specs=(IN_VMEM,) * ways,
        scratch_shapes=[pltpu.VMEM((rows, total), jnp.float32)] * 2,
        compiler_params=pltpu.CompilerParams(vmem_limit_bytes=16 << 20),
    )(place, order, stats, *corrs, *squares)


def split_kernel(ways, count, place, *refs):
    ins, outs, held = refs[:count], refs[count:-1], refs[-1]
    total = ins[0][...]
    for ref in ins[1:]:
        total = total + ref[...]
    held[...] = total
    part = (held.shape[1] - LANE) // ways
    for shift in range(ways):
        start = pl.multiple_of(lax.rem(place[0] + shift, ways) * part, LANE)
        outs[shift][:, 0:part] = held[:, pl.ds(start, part)]
        outs[shift][:, part:] = held[:, part * ways :]


def split_call(place, parts, ways):
    rows, width = parts[0].shape
    shape = jax.ShapeDtypeStruct((rows, (width - LANE) // ways + LANE), jnp.float32)
    return pl.pallas_call(
        functools.partial(split_kernel, ways, len(parts)),
        out_shape=(shape,) * ways,
        in_specs=[pl.BlockSpec(memory_space=pltpu.SMEM)] + [IN_VMEM] * len(parts),
        out_specs=(IN_VMEM,) * ways,
        scratch_shapes=[pltpu.VMEM((rows, width), jnp.float32)],
        compiler_params=pltpu.CompilerParams(vmem_limit_bytes=16 << 20),
    )(place, *parts)


def score_kernel(span, count, *refs):
    ins, out = refs[:count], refs[count]
    total = ins[0][...]
    for ref in ins[1:]:
        total = total + ref[...]
    rows, width = out.shape
    template_energy = total[0:rows, width : width + 1]
    active_count = total[rows:, width : width + 1]
    factor = jnp.sqrt(span * active_count)
    energy = total[rows:, 0:width]
    out[...] = total[0:rows, 0:width] * factor / jnp.sqrt(energy * template_energy + EPSILON)


def score_call(parts, span):
    rows, width = parts[0].shape
    return pl.pallas_call(
        functools.partial(score_kernel, span, len(parts)),
        out_shape=jax.ShapeDtypeStruct((rows // 2, width - LANE), jnp.float32),
        in_specs=[IN_VMEM] * len(parts),
        out_specs=IN_VMEM,
        compiler_params=pltpu.CompilerParams(vmem_limit_bytes=16 << 20),
    )(*parts)


def exchange(parts, axis):
    return [parts[0]] + [shifted(part, axis, shift) for shift, part in enumerate(parts) if shift]


def paired(x, axis, bit):
    return lax.ppermute(x, axis, [(i, i ^ bit) for i in range(lax.axis_size(axis))])


def relays(circle, ways):
    return circle == ways == 4


def relayed_sums(traces, weights, active, stats, sub_place, order, span, ways):
    half = traces.shape[1] // 2
    fars = [paired(traces[:, :half], "tm", 2)]
    fars.append(paired(traces[:, half:], "tm", 2))
    near = paired(traces, "tm", 1)
    before, part = [paired(far, "tm", 1) for far in fars]
    odd = (lax.axis_index("tm") % 2).astype(jnp.int32)[None]
    early = early_call(odd, stats, weights, active, traces, near, fars, span)
    middle = middle_call(weights, active, before, early[3], early[4], span)
    return late_call(sub_place, order, weights, active, before, part, early, middle, span, ways)


def routes(circle, chan_ways, sub_ways):
    held = circle // (chan_ways * sub_ways)
    table = []
    for place in range(circle):
        chan, sub = divmod(place // held, sub_ways)
        slots = [(s, c, h) for s in range(sub_ways) for c in range(chan_ways) for h in range(held)]
        tiles = sorted(range(circle), key=lambda t: -abs(t - place))
        ranked = sorted(range(circle), key=lambda k: (slots[k][1] != chan, slots[k][0] == sub))
        row = [0] * circle
        for slot, time_tile in zip(ranked, tiles):
            row[slot] = time_tile
        table.append(row)
    return table


def gathered_sums(traces, weights, active, stats, sub_place, order, span, ways):
    circle = lax.axis_size("tm")
    arrived = {0: traces}
    for hop in range(1, circle // 2 + 1):
        for near in dict.fromkeys((hop, circle - hop)):
            arrived[near] = shifted(traces, "tm", -near)
    corrs, squares = [], []
    for pair in range(circle // 2):
        first, second = arrived[(2 * pair - 1) % circle], arrived[2 * pair]
        head = arrived[(2 * pair + 1) % circle]
        corr, square = pair_call(weights, active, first, second, head, span)
        corrs.append(corr)
        squares.append(square)
    stats = jnp.broadcast_to(stats, (stats.shape[0], LANE))
    return pack_call(sub_place, order, stats, corrs, squares, span, ways)


def on_device(traces, templates, channel_mask):
    tile = traces.shape[1]
    rows, _, span = templates.shape
    circle = lax.axis_size("tm")
    chan_ways, sub_ways = lax.axis_size("chan"), lax.axis_size("sub")
    active = channel_mask.astype(jnp.bfloat16)
    masked = templates * active[:, :, None]
    weights = arrange(masked, span)
    wide = masked.astype(jnp.float32)
    template_energy = jnp.sum(wide * wide, axis=(1, 2))
    active_count = jnp.sum(channel_mask, axis=1).astype(jnp.float32)
    stats = jnp.concatenate([template_energy, active_count])[:, None]
    sub_place = lax.axis_index("sub").astype(jnp.int32)[None]
    chan_place = lax.axis_index("chan").astype(jnp.int32)[None]

    ways = chan_ways * sub_ways
    held = circle // ways
    relayed = relays(circle, ways)
    if relayed:
        table = routes(circle, chan_ways, sub_ways)
        order = (jnp.array(table, jnp.int32)[lax.axis_index("tm")] + lax.axis_index("tm")) % circle
    else:
        table = [[(slot + place) % circle for slot in range(circle)] for place in range(circle)]
        order = jnp.arange(circle, dtype=jnp.int32)
    sums = relayed_sums if relayed else gathered_sums
    parts = sums(traces, weights, active, stats, sub_place, order.astype(jnp.int32), span, sub_ways)
    parts = exchange(parts, "sub")
    parts = exchange(split_call(chan_place, parts, chan_ways), "chan")
    scores = score_call(parts, span)

    received = []
    for piece in range(held):
        pairs = []
        for place in range(circle):
            for chan in range(chan_ways):
                for sub in range(sub_ways):
                    source = (place * chan_ways + chan) * sub_ways + sub
                    slot = (sub * chan_ways + chan) * held + piece
                    pairs.append((source, table[place][slot] * ways + place // held))
        block = scores[:, piece * tile : (piece + 1) * tile]
        received.append(lax.ppermute(block, ("tm", "chan", "sub"), pairs))
    if held == 1:
        return received[0]
    turn = (lax.axis_index("tm") - jnp.arange(held)) % held
    return jnp.stack(received)[turn].reshape(held * rows, tile)


def solution(mesh):
    placed = (
        P(("chan", "sub"), ("groups", "tm")),
        P("tm", ("chan", "sub"), None),
        P("tm", ("chan", "sub")),
    )
    return jax.shard_map(
        on_device,
        mesh=mesh,
        in_specs=placed,
        out_specs=P(("chan", "sub"), ("groups", "tm")),
        check_vma=False,
    )
```

```python
import functools

import jax
import jax.numpy as jnp
from jax import lax
from jax.experimental import pallas as pl
from jax.experimental.pallas import tpu as pltpu
from jax.sharding import PartitionSpec as P


EPSILON = 1e-06
LANE = 128
FRAMES = 4
STEP = LANE // FRAMES
IN_VMEM = pl.BlockSpec(memory_space=pltpu.VMEM)


def shifted(x, axis, by):
    count = lax.axis_size(axis)
    return lax.ppermute(x, axis, [(i, (i + by) % count) for i in range(count)])


def arrange(masked, span):
    rows, chans, _ = masked.shape
    split = masked.reshape(rows, chans, span // LANE, FRAMES, STEP)
    return split.transpose(2, 4, 0, 3, 1).reshape(span * rows // FRAMES, FRAMES * chans)


def correlate(weights, signal, frames, partial, rows, width):
    chans = signal.shape[0]
    depth = STEP * rows
    blocks = weights.shape[0] // depth
    extent = width + LANE
    reach = extent + (blocks - 1) * LANE
    signal = jnp.concatenate(
        [signal, jnp.zeros((chans, reach + LANE - signal.shape[1]), signal.dtype)], 1
    )
    for frame in range(FRAMES):
        frames[frame * chans : (frame + 1) * chans, :] = signal[:, frame * STEP : frame * STEP + reach]
    total = None
    for block in range(blocks):
        term = jnp.dot(
            weights[block * depth : (block + 1) * depth, :],
            frames[:, block * LANE : block * LANE + extent],
            preferred_element_type=jnp.float32,
        )
        total = term if total is None else total + term
    partial[...] = total
    result = partial[0:rows, 0:width]
    for lag in range(1, STEP):
        result = result + partial[lag * rows : (lag + 1) * rows, lag : lag + width]
    return result


def correlate_alone(weights, part, frames, partial, rows):
    chans, width = part.shape
    depth = STEP * rows
    blocks = weights.shape[0] // depth
    extent = width + LANE
    gap = jnp.zeros((chans, LANE), part.dtype)
    signal = jnp.concatenate([gap, part, gap], 1)
    for frame in range(FRAMES):
        frames[frame * chans : (frame + 1) * chans, :] = signal[:, frame * STEP : frame * STEP + extent]
    partial[...] = jnp.dot(weights[...], frames[...], preferred_element_type=jnp.float32)
    span = blocks * LANE
    result = None
    for lag in range(STEP):
        row = None
        for block in range(blocks):
            first = block * depth + lag * rows
            ends = span - LANE - block * LANE, block * LANE
            pieces = [partial[first : first + rows, :]]
            if ends[0]:
                pieces.insert(0, jnp.zeros((rows, ends[0]), jnp.float32))
            if ends[1]:
                pieces.append(jnp.zeros((rows, ends[1]), jnp.float32))
            piece = jnp.concatenate(pieces, 1)
            row = piece if row is None else row + piece
        row = pltpu.roll(row, span + width - lag, 1) if lag else row
        result = row if result is None else result + row
    return result


def channel_squares(active, signal):
    wide = signal.astype(jnp.float32)
    squares = wide * wide
    high = squares.astype(jnp.bfloat16)
    low = (squares - high.astype(jnp.float32)).astype(jnp.bfloat16)
    return jnp.dot(
        jnp.concatenate([active, active], 1),
        jnp.concatenate([high, low], 0),
        preferred_element_type=jnp.float32,
    )


def pair_kernel(span, weights, active, first, second, head, corr, squares, frames, partial):
    rows, width = corr.shape
    signal = jnp.concatenate([first[...], second[...], head[:, :span]], 1)
    corr[...] = correlate(weights, signal, frames, partial, rows, width)
    squares[...] = channel_squares(active[...], signal[:, :width])


def pair_scratch(chans, rows, width, span):
    extent = width + LANE
    return [
        pltpu.VMEM((FRAMES * chans, extent + span - LANE), jnp.bfloat16),
        pltpu.VMEM((STEP * rows, extent), jnp.float32),
    ]


def pair_call(weights, active, first, second, head, span):
    rows, chans = active.shape
    width = 2 * first.shape[1]
    shape = jax.ShapeDtypeStruct((rows, width), jnp.float32)
    flops = 2 * weights.shape[0] * weights.shape[1] * (width + LANE)
    return pl.pallas_call(
        functools.partial(pair_kernel, span),
        out_shape=(shape, shape),
        in_specs=[IN_VMEM] * 5,
        out_specs=(IN_VMEM, IN_VMEM),
        scratch_shapes=pair_scratch(chans, rows, width, span),
        cost_estimate=pl.CostEstimate(flops=flops, bytes_accessed=1 << 20, transcendentals=0),
        compiler_params=pltpu.CompilerParams(vmem_limit_bytes=32 << 20),
    )(weights, active, first, second, head)


def outer_kernel(span, odd, weights, active, own, *refs):
    fars, (corr, energy, edges, squares, frames, partial) = refs[:-6], refs[-6:]
    rows, width = corr.shape
    width //= 2
    swap = odd[0] == 1
    far = jnp.concatenate([ref[...] for ref in fars], 1)
    for side, tile in enumerate((jnp.where(swap, far, own[...]), jnp.where(swap, own[...], far))):
        columns = slice(side * width, (side + 1) * width)
        corr[:, columns] = correlate(weights, tile, frames, partial, rows, width)
        sums = channel_squares(active[...], tile)
        energy[:, columns] = line_sums(sums, span)[:, :width]
        head, tail = slice(side * span, (side + 1) * span), slice((2 + side) * span, (3 + side) * span)
        edges[:, head], squares[:, head] = tile[:, :span], sums[:, :span]
        edges[:, tail], squares[:, tail] = tile[:, width:], sums[:, width:]


def outer_call(odd, weights, active, own, fars, span):
    rows, chans = active.shape
    width = own.shape[1] - span
    flops = 2 * weights.shape[0] * weights.shape[1] * 2 * width
    shape = jax.ShapeDtypeStruct((rows, 2 * width), jnp.float32)
    return pl.pallas_call(
        functools.partial(outer_kernel, span),
        out_shape=(
            shape,
            shape,
            jax.ShapeDtypeStruct((chans, 4 * span), own.dtype),
            jax.ShapeDtypeStruct((rows, 4 * span), jnp.float32),
        ),
        in_specs=[pl.BlockSpec(memory_space=pltpu.SMEM)] + [IN_VMEM] * (3 + len(fars)),
        out_specs=(IN_VMEM,) * 4,
        scratch_shapes=pair_scratch(chans, rows, width, span),
        cost_estimate=pl.CostEstimate(flops=flops, bytes_accessed=1 << 20, transcendentals=0),
        compiler_params=pltpu.CompilerParams(vmem_limit_bytes=32 << 20),
    )(odd, weights, active, own, *fars)


def inner_kernel(span, weights, active, near, edges, squares, corr, energy, frames, partial):
    rows, width = corr.shape
    before, after = slice(2 * span, 3 * span), slice(span, 2 * span)
    signal = jnp.concatenate([edges[:, before], near[...], edges[:, after]], 1)
    sums = channel_squares(active[...], near[...])
    sums = jnp.concatenate([squares[:, before], sums, squares[:, after]], 1)
    energy[...] = line_sums(sums, span)[:, :width]
    corr[...] = correlate(weights, signal, frames, partial, rows, width)


def inner_call(weights, active, near, edges, squares, span):
    rows, chans = active.shape
    width = span + near.shape[1]
    flops = 2 * weights.shape[0] * weights.shape[1] * width
    shape = jax.ShapeDtypeStruct((rows, width), jnp.float32)
    return pl.pallas_call(
        functools.partial(inner_kernel, span),
        out_shape=(shape, shape),
        in_specs=[IN_VMEM] * 5,
        out_specs=(IN_VMEM,) * 2,
        scratch_shapes=pair_scratch(chans, rows, width, span),
        cost_estimate=pl.CostEstimate(flops=flops, bytes_accessed=1 << 20, transcendentals=0),
        compiler_params=pltpu.CompilerParams(vmem_limit_bytes=32 << 20),
    )(weights, active, near, edges, squares)


def middle_kernel(span, missing, weights, active, part, edges, squares, corr, energy, frames, partial):
    rows, width = corr.shape
    gap = jnp.zeros((part.shape[0], missing), part.dtype)
    before, after = slice(3 * span, 4 * span), slice(0, span)
    signal = jnp.concatenate([edges[:, before], part[...], gap, edges[:, after]], 1)
    sums = channel_squares(active[...], part[...])
    gap = jnp.zeros((rows, missing), jnp.float32)
    sums = jnp.concatenate([squares[:, before], sums, gap, squares[:, after]], 1)
    energy[...] = line_sums(sums, span)[:, :width]
    corr[...] = correlate(weights, signal, frames, partial, rows, width)


def middle_call(weights, active, part, edges, squares, missing, span):
    rows, chans = active.shape
    width = span + part.shape[1] + missing
    flops = 2 * weights.shape[0] * weights.shape[1] * width
    shape = jax.ShapeDtypeStruct((rows, width), jnp.float32)
    return pl.pallas_call(
        functools.partial(middle_kernel, span, missing),
        out_shape=(shape, shape),
        in_specs=[IN_VMEM] * 5,
        out_specs=(IN_VMEM,) * 2,
        scratch_shapes=pair_scratch(chans, rows, width, span),
        cost_estimate=pl.CostEstimate(flops=flops, bytes_accessed=1 << 20, transcendentals=0),
        compiler_params=pltpu.CompilerParams(vmem_limit_bytes=32 << 20),
    )(weights, active, part, edges, squares)


def late_kernel(span, ways, place, order, weights, active, part, outer_corr, outer_energy, inner_corr, inner_energy, middle_corr, middle_energy, *refs):
    outs, (corr_all, energy_all, frames, partial) = refs[:ways], refs[ways:]
    rows, total = corr_all.shape
    side, inner = outer_corr.shape[1] // 2, inner_corr.shape[1]
    start = total - span - part.shape[1]
    kept = start - 2 * side - inner
    sums = channel_squares(active[...], part[...])
    sums = line_sums(jnp.concatenate([jnp.zeros((rows, span), jnp.float32), sums], 1), span)
    alone = correlate_alone(weights, part[...], frames, partial, rows)
    for whole, outer, between, middle, added in (
        (energy_all, outer_energy, inner_energy, middle_energy, sums),
        (corr_all, outer_corr, inner_corr, middle_corr, alone),
    ):
        whole[:, :side] = outer[:, :side]
        whole[:, side : side + inner] = between[...]
        whole[:, side + inner : 2 * side + inner] = outer[:, side:]
        whole[:, start - kept : start] = middle[:, :kept]
        whole[:, start:] = middle[:, kept:] + added
    share(place, order, total // order.shape[0], corr_all, energy_all, outs)


def late_call(place, order, weights, active, part, early, middle, span, ways):
    rows = active.shape[0]
    chans, width = part.shape
    total = sum(early[index].shape[1] for index in (0, 2)) + middle[0].shape[1]
    shape = jax.ShapeDtypeStruct((2 * rows, total // ways), jnp.float32)
    flops = 2 * weights.shape[0] * weights.shape[1] * width
    return pl.pallas_call(
        functools.partial(late_kernel, span, ways),
        out_shape=(shape,) * ways,
        in_specs=[pl.BlockSpec(memory_space=pltpu.SMEM)] * 2 + [IN_VMEM] * (3 + len(early) + len(middle)),
        out_specs=(IN_VMEM,) * ways,
        scratch_shapes=[pltpu.VMEM((rows, total), jnp.float32)] * 2
        + [
            pltpu.VMEM((FRAMES * chans, width + LANE), jnp.bfloat16),
            pltpu.VMEM((weights.shape[0], width + LANE), jnp.float32),
        ],
        cost_estimate=pl.CostEstimate(flops=flops, bytes_accessed=1 << 20, transcendentals=0),
        compiler_params=pltpu.CompilerParams(vmem_limit_bytes=32 << 20),
    )(place, order, weights, active, part, *early, *middle)


def share(place, order, tile, corr_all, energy_all, outs):
    rows, total = corr_all.shape
    ways = len(outs)
    count = total // tile // ways
    for shift in range(ways):
        group = lax.rem(place[0] + shift, ways) * count
        for item in range(count):
            start = pl.multiple_of(order[group + item] * tile, LANE)
            columns = slice(item * tile, (item + 1) * tile)
            outs[shift][0:rows, columns] = corr_all[:, pl.ds(start, tile)]
            outs[shift][rows : 2 * rows, columns] = energy_all[:, pl.ds(start, tile)]


def line_sums(values, span):
    reach = 1
    while reach < span:
        values = values + jnp.concatenate([values[:, reach:], values[:, :reach]], 1)
        reach *= 2
    return values


def pack_kernel(span, tile, pairs, place, order, *refs):
    corrs, squares = refs[:pairs], refs[pairs : 2 * pairs]
    outs, corr_all, energy_all = refs[2 * pairs : -2], refs[-2], refs[-1]
    corr = jnp.concatenate([ref[...] for ref in corrs], 1)
    corr_all[...] = jnp.concatenate([corr[:, tile:], corr[:, :tile]], 1)
    energy = line_sums(jnp.concatenate([ref[...] for ref in squares], 1), span)
    energy_all[...] = jnp.concatenate([energy[:, tile:], energy[:, :tile]], 1)
    share(place, order, tile, corr_all, energy_all, outs)


def pack_call(place, order, corrs, squares, span, ways):
    rows, width = corrs[0].shape
    pairs = len(corrs)
    total = pairs * width
    shape = jax.ShapeDtypeStruct((2 * rows, total // ways), jnp.float32)
    return pl.pallas_call(
        functools.partial(pack_kernel, span, width // 2, pairs),
        out_shape=(shape,) * ways,
        in_specs=[pl.BlockSpec(memory_space=pltpu.SMEM)] * 2 + [IN_VMEM] * (2 * pairs),
        out_specs=(IN_VMEM,) * ways,
        scratch_shapes=[pltpu.VMEM((rows, total), jnp.float32)] * 2,
        compiler_params=pltpu.CompilerParams(vmem_limit_bytes=16 << 20),
    )(place, order, *corrs, *squares)


def split_kernel(ways, count, place, *refs):
    ins, outs, held = refs[:count], refs[count:-1], refs[-1]
    total = ins[0][...]
    for ref in ins[1:]:
        total = total + ref[...]
    held[...] = total
    part = held.shape[1] // ways
    for shift in range(ways):
        start = pl.multiple_of(lax.rem(place[0] + shift, ways) * part, LANE)
        outs[shift][...] = held[:, pl.ds(start, part)]


def split_call(place, parts, ways):
    rows, width = parts[0].shape
    shape = jax.ShapeDtypeStruct((rows, width // ways), jnp.float32)
    return pl.pallas_call(
        functools.partial(split_kernel, ways, len(parts)),
        out_shape=(shape,) * ways,
        in_specs=[pl.BlockSpec(memory_space=pltpu.SMEM)] + [IN_VMEM] * len(parts),
        out_specs=(IN_VMEM,) * ways,
        scratch_shapes=[pltpu.VMEM((rows, width), jnp.float32)],
        compiler_params=pltpu.CompilerParams(vmem_limit_bytes=16 << 20),
    )(place, *parts)


def score_kernel(span, count, stats, *refs):
    ins, out = refs[:count], refs[count]
    total = ins[0][...]
    for ref in ins[1:]:
        total = total + ref[...]
    rows = out.shape[0]
    template_energy = stats[0:rows, 0:1]
    active_count = stats[rows:, 0:1]
    factor = jnp.sqrt(span * active_count)
    energy = total[rows:, :]
    out[...] = total[0:rows, :] * factor / jnp.sqrt(energy * template_energy + EPSILON)


def score_call(stats, parts, span):
    rows, width = parts[0].shape
    return pl.pallas_call(
        functools.partial(score_kernel, span, len(parts)),
        out_shape=jax.ShapeDtypeStruct((rows // 2, width), jnp.float32),
        in_specs=[IN_VMEM] * (1 + len(parts)),
        out_specs=IN_VMEM,
        compiler_params=pltpu.CompilerParams(vmem_limit_bytes=16 << 20),
    )(stats, *parts)


def exchange(parts, axis):
    return [parts[0]] + [shifted(part, axis, shift) for shift, part in enumerate(parts) if shift]


def paired(x, axis, bit):
    return lax.ppermute(x, axis, [(i, i ^ bit) for i in range(lax.axis_size(axis))])


def relays(circle, ways):
    return circle == ways == 4


def relayed_sums(traces, weights, active, sub_place, order, span, ways):
    half = traces.shape[1] // 2
    fars = [paired(traces[:, :half], "tm", 2)]
    fars.append(paired(traces[:, half:], "tm", 2))
    near = paired(traces, "tm", 1)
    before = paired(fars[0], "tm", 1)
    part = paired(fars[1], "tm", 1)
    odd = (lax.axis_index("tm") % 2).astype(jnp.int32)[None]
    *outer, edges, squares = outer_call(odd, weights, active, traces, fars, span)
    early = (*outer, *inner_call(weights, active, near, edges, squares, span))
    middle = middle_call(weights, active, before, edges, squares, part.shape[1], span)
    return late_call(sub_place, order, weights, active, part, early, middle, span, ways)


def routes(circle, chan_ways, sub_ways):
    held = circle // (chan_ways * sub_ways)
    table = []
    for place in range(circle):
        chan = place // held // sub_ways
        slots = [(s, c, h) for s in range(sub_ways) for c in range(chan_ways) for h in range(held)]
        tiles = sorted(range(circle), key=lambda t: -abs(t - place))
        ranked = sorted(range(circle), key=lambda k: (slots[k][1] != chan, -slots[k][0]))
        row = [0] * circle
        for slot, time_tile in zip(ranked, tiles):
            row[slot] = time_tile
        table.append(row)
    return table


def gathered_sums(traces, weights, active, sub_place, order, span, ways):
    circle = lax.axis_size("tm")
    arrived = {0: traces}
    for hop in range(1, circle // 2 + 1):
        for near in dict.fromkeys((hop, circle - hop)):
            arrived[near] = shifted(traces, "tm", -near)
    corrs, squares = [], []
    for pair in range(circle // 2):
        first, second = arrived[(2 * pair - 1) % circle], arrived[2 * pair]
        head = arrived[(2 * pair + 1) % circle]
        corr, square = pair_call(weights, active, first, second, head, span)
        corrs.append(corr)
        squares.append(square)
    return pack_call(sub_place, order, corrs, squares, span, ways)


def on_device(traces, templates, channel_mask):
    tile = traces.shape[1]
    rows, _, span = templates.shape
    circle = lax.axis_size("tm")
    chan_ways, sub_ways = lax.axis_size("chan"), lax.axis_size("sub")
    active = channel_mask.astype(jnp.bfloat16)
    masked = templates * active[:, :, None]
    weights = arrange(masked, span)
    wide = masked.astype(jnp.float32)
    template_energy = jnp.sum(wide * wide, axis=(1, 2))
    active_count = jnp.sum(channel_mask, axis=1).astype(jnp.float32)
    stats = jnp.broadcast_to(jnp.concatenate([template_energy, active_count])[:, None], (2 * rows, LANE))
    for axis in ("sub", "chan"):
        others = [shifted(stats, axis, by) for by in range(1, lax.axis_size(axis))]
        stats = sum(others, stats)
    sub_place = lax.axis_index("sub").astype(jnp.int32)[None]
    chan_place = lax.axis_index("chan").astype(jnp.int32)[None]

    ways = chan_ways * sub_ways
    held = circle // ways
    relayed = relays(circle, ways)
    if relayed:
        table = routes(circle, chan_ways, sub_ways)
        order = (jnp.array(table, jnp.int32)[lax.axis_index("tm")] + lax.axis_index("tm")) % circle
    else:
        table = [[(slot + place) % circle for slot in range(circle)] for place in range(circle)]
        order = jnp.arange(circle, dtype=jnp.int32)
    sums = relayed_sums if relayed else gathered_sums
    parts = sums(traces, weights, active, sub_place, order.astype(jnp.int32), span, sub_ways)
    parts = exchange(parts, "sub")
    parts = exchange(split_call(chan_place, parts, chan_ways), "chan")
    scores = score_call(stats, parts, span)

    received = []
    for piece in range(held):
        pairs = []
        for place in range(circle):
            for chan in range(chan_ways):
                for sub in range(sub_ways):
                    source = (place * chan_ways + chan) * sub_ways + sub
                    slot = (sub * chan_ways + chan) * held + piece
                    pairs.append((source, table[place][slot] * ways + place // held))
        block = scores[:, piece * tile : (piece + 1) * tile]
        received.append(lax.ppermute(block, ("tm", "chan", "sub"), pairs))
    if held == 1:
        return received[0]
    turn = (lax.axis_index("tm") - jnp.arange(held)) % held
    return jnp.stack(received)[turn].reshape(held * rows, tile)


def solution(mesh):
    placed = (
        P(("chan", "sub"), ("groups", "tm")),
        P("tm", ("chan", "sub"), None),
        P("tm", ("chan", "sub")),
    )
    return jax.shard_map(
        on_device,
        mesh=mesh,
        in_specs=placed,
        out_specs=P(("chan", "sub"), ("groups", "tm")),
        check_vma=False,
    )
```

```python
import functools

import jax
import jax.numpy as jnp
from jax import lax
from jax.experimental import pallas as pl
from jax.experimental.pallas import tpu as pltpu
from jax.sharding import PartitionSpec as P


EPSILON = 1e-06
LANE = 128
FRAMES = 4
STEP = LANE // FRAMES
IN_VMEM = pl.BlockSpec(memory_space=pltpu.VMEM)


def shifted(x, axis, by):
    count = lax.axis_size(axis)
    return lax.ppermute(x, axis, [(i, (i + by) % count) for i in range(count)])


def arrange(masked, span):
    rows, chans, _ = masked.shape
    split = masked.reshape(rows, chans, span // LANE, FRAMES, STEP)
    return split.transpose(2, 4, 0, 3, 1).reshape(span * rows // FRAMES, FRAMES * chans)


def correlate(weights, signal, frames, partial, rows, width):
    chans = signal.shape[0]
    depth = STEP * rows
    blocks = weights.shape[0] // depth
    extent = width + LANE
    reach = extent + (blocks - 1) * LANE
    signal = jnp.concatenate(
        [signal, jnp.zeros((chans, reach + LANE - signal.shape[1]), signal.dtype)], 1
    )
    for frame in range(FRAMES):
        frames[frame * chans : (frame + 1) * chans, :] = signal[:, frame * STEP : frame * STEP + reach]
    total = None
    for block in range(blocks):
        term = jnp.dot(
            weights[block * depth : (block + 1) * depth, :],
            frames[:, block * LANE : block * LANE + extent],
            preferred_element_type=jnp.float32,
        )
        total = term if total is None else total + term
    partial[...] = total
    result = partial[0:rows, 0:width]
    for lag in range(1, STEP):
        result = result + partial[lag * rows : (lag + 1) * rows, lag : lag + width]
    return result


def correlate_alone(weights, part, frames, partial, rows):
    chans, width = part.shape
    depth = STEP * rows
    blocks = weights.shape[0] // depth
    extent = width + LANE
    gap = jnp.zeros((chans, LANE), part.dtype)
    signal = jnp.concatenate([gap, part, gap], 1)
    for frame in range(FRAMES):
        frames[frame * chans : (frame + 1) * chans, :] = signal[:, frame * STEP : frame * STEP + extent]
    partial[...] = jnp.dot(weights[...], frames[...], preferred_element_type=jnp.float32)
    span = blocks * LANE
    result = None
    for lag in range(STEP):
        row = None
        for block in range(blocks):
            first = block * depth + lag * rows
            ends = span - LANE - block * LANE, block * LANE
            pieces = [partial[first : first + rows, :]]
            if ends[0]:
                pieces.insert(0, jnp.zeros((rows, ends[0]), jnp.float32))
            if ends[1]:
                pieces.append(jnp.zeros((rows, ends[1]), jnp.float32))
            piece = jnp.concatenate(pieces, 1)
            row = piece if row is None else row + piece
        row = pltpu.roll(row, span + width - lag, 1) if lag else row
        result = row if result is None else result + row
    return result


def channel_squares(active, signal):
    wide = signal.astype(jnp.float32)
    squares = wide * wide
    high = squares.astype(jnp.bfloat16)
    low = (squares - high.astype(jnp.float32)).astype(jnp.bfloat16)
    return jnp.dot(
        jnp.concatenate([active, active], 1),
        jnp.concatenate([high, low], 0),
        preferred_element_type=jnp.float32,
    )


def pair_kernel(span, weights, active, first, second, head, corr, squares, frames, partial):
    rows, width = corr.shape
    signal = jnp.concatenate([first[...], second[...], head[:, :span]], 1)
    corr[...] = correlate(weights, signal, frames, partial, rows, width)
    squares[...] = channel_squares(active[...], signal[:, :width])


def pair_scratch(chans, rows, width, span):
    extent = width + LANE
    return [
        pltpu.VMEM((FRAMES * chans, extent + span - LANE), jnp.bfloat16),
        pltpu.VMEM((STEP * rows, extent), jnp.float32),
    ]


def pair_call(weights, active, first, second, head, span):
    rows, chans = active.shape
    width = 2 * first.shape[1]
    shape = jax.ShapeDtypeStruct((rows, width), jnp.float32)
    flops = 2 * weights.shape[0] * weights.shape[1] * (width + LANE)
    return pl.pallas_call(
        functools.partial(pair_kernel, span),
        out_shape=(shape, shape),
        in_specs=[IN_VMEM] * 5,
        out_specs=(IN_VMEM, IN_VMEM),
        scratch_shapes=pair_scratch(chans, rows, width, span),
        cost_estimate=pl.CostEstimate(flops=flops, bytes_accessed=1 << 20, transcendentals=0),
        compiler_params=pltpu.CompilerParams(vmem_limit_bytes=32 << 20),
    )(weights, active, first, second, head)


def outer_kernel(span, odd, weights, active, own, *refs):
    fars, (corr, energy, edges, squares, frames, partial) = refs[:-6], refs[-6:]
    rows, width = corr.shape
    width //= 2
    swap = odd[0] == 1
    far = jnp.concatenate([ref[...] for ref in fars], 1)
    for side, tile in enumerate((jnp.where(swap, far, own[...]), jnp.where(swap, own[...], far))):
        columns = slice(side * width, (side + 1) * width)
        corr[:, columns] = correlate(weights, tile, frames, partial, rows, width)
        sums = channel_squares(active[...], tile)
        energy[:, columns] = line_sums(sums, span)[:, :width]
        head, tail = slice(side * span, (side + 1) * span), slice((2 + side) * span, (3 + side) * span)
        edges[:, head], squares[:, head] = tile[:, :span], sums[:, :span]
        edges[:, tail], squares[:, tail] = tile[:, width:], sums[:, width:]


def outer_call(odd, weights, active, own, fars, span):
    rows, chans = active.shape
    width = own.shape[1] - span
    flops = 2 * weights.shape[0] * weights.shape[1] * 2 * width
    shape = jax.ShapeDtypeStruct((rows, 2 * width), jnp.float32)
    return pl.pallas_call(
        functools.partial(outer_kernel, span),
        out_shape=(
            shape,
            shape,
            jax.ShapeDtypeStruct((chans, 4 * span), own.dtype),
            jax.ShapeDtypeStruct((rows, 4 * span), jnp.float32),
        ),
        in_specs=[pl.BlockSpec(memory_space=pltpu.SMEM)] + [IN_VMEM] * (3 + len(fars)),
        out_specs=(IN_VMEM,) * 4,
        scratch_shapes=pair_scratch(chans, rows, width, span),
        cost_estimate=pl.CostEstimate(flops=flops, bytes_accessed=1 << 20, transcendentals=0),
        compiler_params=pltpu.CompilerParams(vmem_limit_bytes=32 << 20),
    )(odd, weights, active, own, *fars)


def inner_kernel(span, weights, active, near, edges, squares, corr, energy, frames, partial):
    rows, width = corr.shape
    before, after = slice(2 * span, 3 * span), slice(span, 2 * span)
    signal = jnp.concatenate([edges[:, before], near[...], edges[:, after]], 1)
    sums = channel_squares(active[...], near[...])
    sums = jnp.concatenate([squares[:, before], sums, squares[:, after]], 1)
    energy[...] = line_sums(sums, span)[:, :width]
    corr[...] = correlate(weights, signal, frames, partial, rows, width)


def inner_call(weights, active, near, edges, squares, span):
    rows, chans = active.shape
    width = span + near.shape[1]
    flops = 2 * weights.shape[0] * weights.shape[1] * width
    shape = jax.ShapeDtypeStruct((rows, width), jnp.float32)
    return pl.pallas_call(
        functools.partial(inner_kernel, span),
        out_shape=(shape, shape),
        in_specs=[IN_VMEM] * 5,
        out_specs=(IN_VMEM,) * 2,
        scratch_shapes=pair_scratch(chans, rows, width, span),
        cost_estimate=pl.CostEstimate(flops=flops, bytes_accessed=1 << 20, transcendentals=0),
        compiler_params=pltpu.CompilerParams(vmem_limit_bytes=32 << 20),
    )(weights, active, near, edges, squares)


def middle_kernel(span, missing, weights, active, part, edges, squares, corr, energy, frames, partial):
    rows, width = corr.shape
    gap = jnp.zeros((part.shape[0], missing), part.dtype)
    before, after = slice(3 * span, 4 * span), slice(0, span)
    signal = jnp.concatenate([edges[:, before], part[...], gap, edges[:, after]], 1)
    sums = channel_squares(active[...], part[...])
    gap = jnp.zeros((rows, missing), jnp.float32)
    sums = jnp.concatenate([squares[:, before], sums, gap, squares[:, after]], 1)
    energy[...] = line_sums(sums, span)[:, :width]
    corr[...] = correlate(weights, signal, frames, partial, rows, width)


def middle_call(weights, active, part, edges, squares, missing, span):
    rows, chans = active.shape
    width = span + part.shape[1] + missing
    flops = 2 * weights.shape[0] * weights.shape[1] * width
    shape = jax.ShapeDtypeStruct((rows, width), jnp.float32)
    return pl.pallas_call(
        functools.partial(middle_kernel, span, missing),
        out_shape=(shape, shape),
        in_specs=[IN_VMEM] * 5,
        out_specs=(IN_VMEM,) * 2,
        scratch_shapes=pair_scratch(chans, rows, width, span),
        cost_estimate=pl.CostEstimate(flops=flops, bytes_accessed=1 << 20, transcendentals=0),
        compiler_params=pltpu.CompilerParams(vmem_limit_bytes=32 << 20),
    )(weights, active, part, edges, squares)


def late_kernel(span, ways, table, place, weights, active, part, outer_corr, outer_energy, inner_corr, inner_energy, middle_corr, middle_energy, *refs):
    outs, (corr_all, energy_all, frames, partial) = refs[:ways], refs[ways:]
    rows, total = corr_all.shape
    side, inner = outer_corr.shape[1] // 2, inner_corr.shape[1]
    start = total - span - part.shape[1]
    kept = start - 2 * side - inner
    sums = channel_squares(active[...], part[...])
    sums = line_sums(jnp.concatenate([jnp.zeros((rows, span), jnp.float32), sums], 1), span)
    alone = correlate_alone(weights, part[...], frames, partial, rows)
    for whole, outer, between, middle, added in (
        (energy_all, outer_energy, inner_energy, middle_energy, sums),
        (corr_all, outer_corr, inner_corr, middle_corr, alone),
    ):
        whole[:, :side] = outer[:, :side]
        whole[:, side : side + inner] = between[...]
        whole[:, side + inner : 2 * side + inner] = outer[:, side:]
        whole[:, start - kept : start] = middle[:, :kept]
        whole[:, start:] = middle[:, kept:] + added
    share(place, table, total // len(table), corr_all, energy_all, outs)


def late_call(place, table, weights, active, part, early, middle, span, ways):
    rows = active.shape[0]
    chans, width = part.shape
    total = sum(early[index].shape[1] for index in (0, 2)) + middle[0].shape[1]
    shape = jax.ShapeDtypeStruct((2 * rows, total // ways), jnp.float32)
    flops = 2 * weights.shape[0] * weights.shape[1] * width
    return pl.pallas_call(
        functools.partial(late_kernel, span, ways, table),
        out_shape=(shape,) * ways,
        in_specs=[pl.BlockSpec(memory_space=pltpu.SMEM)] + [IN_VMEM] * (3 + len(early) + len(middle)),
        out_specs=(IN_VMEM,) * ways,
        scratch_shapes=[pltpu.VMEM((rows, total), jnp.float32)] * 2
        + [
            pltpu.VMEM((FRAMES * chans, width + LANE), jnp.bfloat16),
            pltpu.VMEM((weights.shape[0], width + LANE), jnp.float32),
        ],
        cost_estimate=pl.CostEstimate(flops=flops, bytes_accessed=1 << 20, transcendentals=0),
        compiler_params=pltpu.CompilerParams(vmem_limit_bytes=32 << 20),
    )(place, weights, active, part, *early, *middle)


def share(place, table, tile, corr_all, energy_all, outs):
    rows, total = corr_all.shape
    ways = len(outs)
    count = total // tile // ways
    for shift in range(ways):
        group = lax.rem(place[0] + shift, ways) * count
        for item in range(count):
            position = group + item
            if table:
                position = jnp.int32(0)
                for home, row in enumerate(table):
                    for slot, value in enumerate(row):
                        chosen = (place[1] == home) & (group + item == slot)
                        position = jnp.where(chosen, value, position)
            start = pl.multiple_of(position * tile, LANE)
            columns = slice(item * tile, (item + 1) * tile)
            outs[shift][0:rows, columns] = corr_all[:, pl.ds(start, tile)]
            outs[shift][rows : 2 * rows, columns] = energy_all[:, pl.ds(start, tile)]


def line_sums(values, span):
    reach = 1
    while reach < span:
        values = values + jnp.concatenate([values[:, reach:], values[:, :reach]], 1)
        reach *= 2
    return values


def pack_kernel(span, tile, pairs, place, *refs):
    corrs, squares = refs[:pairs], refs[pairs : 2 * pairs]
    outs, corr_all, energy_all = refs[2 * pairs : -2], refs[-2], refs[-1]
    corr = jnp.concatenate([ref[...] for ref in corrs], 1)
    corr_all[...] = jnp.concatenate([corr[:, tile:], corr[:, :tile]], 1)
    energy = line_sums(jnp.concatenate([ref[...] for ref in squares], 1), span)
    energy_all[...] = jnp.concatenate([energy[:, tile:], energy[:, :tile]], 1)
    share(place, None, tile, corr_all, energy_all, outs)


def pack_call(place, corrs, squares, span, ways):
    rows, width = corrs[0].shape
    pairs = len(corrs)
    total = pairs * width
    shape = jax.ShapeDtypeStruct((2 * rows, total // ways), jnp.float32)
    return pl.pallas_call(
        functools.partial(pack_kernel, span, width // 2, pairs),
        out_shape=(shape,) * ways,
        in_specs=[pl.BlockSpec(memory_space=pltpu.SMEM)] + [IN_VMEM] * (2 * pairs),
        out_specs=(IN_VMEM,) * ways,
        scratch_shapes=[pltpu.VMEM((rows, total), jnp.float32)] * 2,
        compiler_params=pltpu.CompilerParams(vmem_limit_bytes=16 << 20),
    )(place, *corrs, *squares)


def split_kernel(ways, count, place, *refs):
    ins, outs, held = refs[:count], refs[count:-1], refs[-1]
    total = ins[0][...]
    for ref in ins[1:]:
        total = total + ref[...]
    held[...] = total
    part = held.shape[1] // ways
    for shift in range(ways):
        start = pl.multiple_of(lax.rem(place[0] + shift, ways) * part, LANE)
        outs[shift][...] = held[:, pl.ds(start, part)]


def split_call(place, parts, ways):
    rows, width = parts[0].shape
    shape = jax.ShapeDtypeStruct((rows, width // ways), jnp.float32)
    return pl.pallas_call(
        functools.partial(split_kernel, ways, len(parts)),
        out_shape=(shape,) * ways,
        in_specs=[pl.BlockSpec(memory_space=pltpu.SMEM)] + [IN_VMEM] * len(parts),
        out_specs=(IN_VMEM,) * ways,
        scratch_shapes=[pltpu.VMEM((rows, width), jnp.float32)],
        compiler_params=pltpu.CompilerParams(vmem_limit_bytes=16 << 20),
    )(place, *parts)


def score_kernel(span, count, stats, *refs):
    ins, out = refs[:count], refs[count]
    total = ins[0][...]
    for ref in ins[1:]:
        total = total + ref[...]
    rows = out.shape[0]
    template_energy = stats[0:rows, 0:1]
    active_count = stats[rows:, 0:1]
    factor = jnp.sqrt(span * active_count)
    energy = total[rows:, :]
    out[...] = total[0:rows, :] * factor / jnp.sqrt(energy * template_energy + EPSILON)


def score_call(stats, parts, span):
    rows, width = parts[0].shape
    return pl.pallas_call(
        functools.partial(score_kernel, span, len(parts)),
        out_shape=jax.ShapeDtypeStruct((rows // 2, width), jnp.float32),
        in_specs=[IN_VMEM] * (1 + len(parts)),
        out_specs=IN_VMEM,
        compiler_params=pltpu.CompilerParams(vmem_limit_bytes=16 << 20),
    )(stats, *parts)


def exchange(parts, axis):
    return [parts[0]] + [shifted(part, axis, shift) for shift, part in enumerate(parts) if shift]


def paired(x, axis, bit):
    return lax.ppermute(x, axis, [(i, i ^ bit) for i in range(lax.axis_size(axis))])


def relays(circle, ways):
    return circle == ways == 4


def relayed_sums(traces, weights, active, place, table, span, ways):
    half = traces.shape[1] // 2
    fars = [paired(traces[:, :half], "tm", 2)]
    fars.append(paired(traces[:, half:], "tm", 2))
    near = paired(traces, "tm", 1)
    before = paired(fars[0], "tm", 1)
    part = paired(fars[1], "tm", 1)
    odd = (lax.axis_index("tm") % 2).astype(jnp.int32)[None]
    *outer, edges, squares = outer_call(odd, weights, active, traces, fars, span)
    early = (*outer, *inner_call(weights, active, near, edges, squares, span))
    middle = middle_call(weights, active, before, edges, squares, part.shape[1], span)
    return late_call(place, table, weights, active, part, early, middle, span, ways)


def routes(circle, chan_ways, sub_ways):
    held = circle // (chan_ways * sub_ways)
    table = []
    for place in range(circle):
        chan = place // held // sub_ways
        slots = [(s, c, h) for s in range(sub_ways) for c in range(chan_ways) for h in range(held)]
        tiles = sorted(range(circle), key=lambda t: -abs(t - place))
        ranked = sorted(range(circle), key=lambda k: (slots[k][1] != chan, -slots[k][0]))
        row = [0] * circle
        for slot, time_tile in zip(ranked, tiles):
            row[slot] = time_tile
        table.append(row)
    return table


def gathered_sums(traces, weights, active, place, table, span, ways):
    circle = lax.axis_size("tm")
    arrived = {0: traces}
    for hop in range(1, circle // 2 + 1):
        for near in dict.fromkeys((hop, circle - hop)):
            arrived[near] = shifted(traces, "tm", -near)
    corrs, squares = [], []
    for pair in range(circle // 2):
        first, second = arrived[(2 * pair - 1) % circle], arrived[2 * pair]
        head = arrived[(2 * pair + 1) % circle]
        corr, square = pair_call(weights, active, first, second, head, span)
        corrs.append(corr)
        squares.append(square)
    return pack_call(place, corrs, squares, span, ways)


def on_device(traces, templates, channel_mask):
    tile = traces.shape[1]
    rows, _, span = templates.shape
    circle = lax.axis_size("tm")
    chan_ways, sub_ways = lax.axis_size("chan"), lax.axis_size("sub")
    active = channel_mask.astype(jnp.bfloat16)
    masked = templates * active[:, :, None]
    weights = arrange(masked, span)
    wide = masked.astype(jnp.float32)
    template_energy = jnp.sum(wide * wide, axis=(1, 2))
    active_count = jnp.sum(channel_mask, axis=1).astype(jnp.float32)
    stats = jnp.broadcast_to(jnp.concatenate([template_energy, active_count])[:, None], (2 * rows, LANE))
    for axis in ("sub", "chan"):
        others = [shifted(stats, axis, by) for by in range(1, lax.axis_size(axis))]
        stats = sum(others, stats)
    place = jnp.stack([lax.axis_index("sub"), lax.axis_index("tm")]).astype(jnp.int32)
    chan_place = lax.axis_index("chan").astype(jnp.int32)[None]

    ways = chan_ways * sub_ways
    held = circle // ways
    relayed = relays(circle, ways)
    if relayed:
        table = routes(circle, chan_ways, sub_ways)
    else:
        table = [[(slot + place) % circle for slot in range(circle)] for place in range(circle)]
    sums = relayed_sums if relayed else gathered_sums
    spots = [[(time_tile + home) % circle for time_tile in row] for home, row in enumerate(table)]
    parts = sums(traces, weights, active, place, spots, span, sub_ways)
    parts = exchange(parts, "sub")
    parts = exchange(split_call(chan_place, parts, chan_ways), "chan")
    scores = score_call(stats, parts, span)

    received = []
    for piece in range(held):
        pairs = []
        for place in range(circle):
            for chan in range(chan_ways):
                for sub in range(sub_ways):
                    source = (place * chan_ways + chan) * sub_ways + sub
                    slot = (sub * chan_ways + chan) * held + piece
                    pairs.append((source, table[place][slot] * ways + place // held))
        block = scores[:, piece * tile : (piece + 1) * tile]
        received.append(lax.ppermute(block, ("tm", "chan", "sub"), pairs))
    if held == 1:
        return received[0]
    turn = (lax.axis_index("tm") - jnp.arange(held)) % held
    return jnp.stack(received)[turn].reshape(held * rows, tile)


def solution(mesh):
    placed = (
        P(("chan", "sub"), ("groups", "tm")),
        P("tm", ("chan", "sub"), None),
        P("tm", ("chan", "sub")),
    )
    return jax.shard_map(
        on_device,
        mesh=mesh,
        in_specs=placed,
        out_specs=P(("chan", "sub"), ("groups", "tm")),
        check_vma=False,
    )
```

```python
import functools

import jax
import jax.numpy as jnp
from jax import lax
from jax.experimental import pallas as pl
from jax.experimental.pallas import tpu as pltpu
from jax.sharding import PartitionSpec as P


EPSILON = 1e-06
LANE = 128
FRAMES = 4
STEP = LANE // FRAMES
IN_VMEM = pl.BlockSpec(memory_space=pltpu.VMEM)


def shifted(x, axis, by):
    count = lax.axis_size(axis)
    return lax.ppermute(x, axis, [(i, (i + by) % count) for i in range(count)])


def arrange(masked, span):
    rows, chans, _ = masked.shape
    split = masked.reshape(rows, chans, span // LANE, FRAMES, STEP)
    return split.transpose(2, 4, 0, 3, 1).reshape(span * rows // FRAMES, FRAMES * chans)


def correlate(weights, signal, frames, partial, rows, width):
    chans = signal.shape[0]
    depth = STEP * rows
    blocks = weights.shape[0] // depth
    extent = width + LANE
    reach = extent + (blocks - 1) * LANE
    signal = jnp.concatenate(
        [signal, jnp.zeros((chans, reach + LANE - signal.shape[1]), signal.dtype)], 1
    )
    for frame in range(FRAMES):
        frames[frame * chans : (frame + 1) * chans, :] = signal[:, frame * STEP : frame * STEP + reach]
    total = None
    for block in range(blocks):
        term = jnp.dot(
            weights[block * depth : (block + 1) * depth, :],
            frames[:, block * LANE : block * LANE + extent],
            preferred_element_type=jnp.float32,
        )
        total = term if total is None else total + term
    partial[...] = total
    result = partial[0:rows, 0:width]
    for lag in range(1, STEP):
        result = result + partial[lag * rows : (lag + 1) * rows, lag : lag + width]
    return result


def correlate_alone(weights, part, frames, partial, rows):
    chans, width = part.shape
    depth = STEP * rows
    blocks = weights.shape[0] // depth
    extent = width + LANE
    gap = jnp.zeros((chans, LANE), part.dtype)
    signal = jnp.concatenate([gap, part, gap], 1)
    for frame in range(FRAMES):
        frames[frame * chans : (frame + 1) * chans, :] = signal[:, frame * STEP : frame * STEP + extent]
    partial[...] = jnp.dot(weights[...], frames[...], preferred_element_type=jnp.float32)
    span = blocks * LANE
    result = None
    for lag in range(STEP):
        row = None
        for block in range(blocks):
            first = block * depth + lag * rows
            ends = span - LANE - block * LANE, block * LANE
            pieces = [partial[first : first + rows, :]]
            if ends[0]:
                pieces.insert(0, jnp.zeros((rows, ends[0]), jnp.float32))
            if ends[1]:
                pieces.append(jnp.zeros((rows, ends[1]), jnp.float32))
            piece = jnp.concatenate(pieces, 1)
            row = piece if row is None else row + piece
        row = pltpu.roll(row, span + width - lag, 1) if lag else row
        result = row if result is None else result + row
    return result


def channel_squares(active, signal):
    wide = signal.astype(jnp.float32)
    squares = wide * wide
    high = squares.astype(jnp.bfloat16)
    low = (squares - high.astype(jnp.float32)).astype(jnp.bfloat16)
    return jnp.dot(
        jnp.concatenate([active, active], 1),
        jnp.concatenate([high, low], 0),
        preferred_element_type=jnp.float32,
    )


def pair_kernel(span, weights, active, first, second, head, corr, squares, frames, partial):
    rows, width = corr.shape
    signal = jnp.concatenate([first[...], second[...], head[:, :span]], 1)
    corr[...] = correlate(weights, signal, frames, partial, rows, width)
    squares[...] = channel_squares(active[...], signal[:, :width])


def pair_scratch(chans, rows, width, span):
    extent = width + LANE
    return [
        pltpu.VMEM((FRAMES * chans, extent + span - LANE), jnp.bfloat16),
        pltpu.VMEM((STEP * rows, extent), jnp.float32),
    ]


def pair_call(weights, active, first, second, head, span):
    rows, chans = active.shape
    width = 2 * first.shape[1]
    shape = jax.ShapeDtypeStruct((rows, width), jnp.float32)
    flops = 2 * weights.shape[0] * weights.shape[1] * (width + LANE)
    return pl.pallas_call(
        functools.partial(pair_kernel, span),
        out_shape=(shape, shape),
        in_specs=[IN_VMEM] * 5,
        out_specs=(IN_VMEM, IN_VMEM),
        scratch_shapes=pair_scratch(chans, rows, width, span),
        cost_estimate=pl.CostEstimate(flops=flops, bytes_accessed=1 << 20, transcendentals=0),
        compiler_params=pltpu.CompilerParams(vmem_limit_bytes=32 << 20),
    )(weights, active, first, second, head)


def outer_kernel(span, odd, weights, active, own, *refs):
    fars, (corr, energy, edges, squares, frames, partial) = refs[:-6], refs[-6:]
    rows, width = corr.shape
    width //= 2
    swap = odd[0] == 1
    far = jnp.concatenate([ref[...] for ref in fars], 1)
    for side, tile in enumerate((jnp.where(swap, far, own[...]), jnp.where(swap, own[...], far))):
        columns = slice(side * width, (side + 1) * width)
        corr[:, columns] = correlate(weights, tile, frames, partial, rows, width)
        sums = channel_squares(active[...], tile)
        energy[:, columns] = line_sums(sums, span)[:, :width]
        head, tail = slice(side * span, (side + 1) * span), slice((2 + side) * span, (3 + side) * span)
        edges[:, head], squares[:, head] = tile[:, :span], sums[:, :span]
        edges[:, tail], squares[:, tail] = tile[:, width:], sums[:, width:]


def outer_call(odd, weights, active, own, fars, span):
    rows, chans = active.shape
    width = own.shape[1] - span
    flops = 2 * weights.shape[0] * weights.shape[1] * 2 * width
    shape = jax.ShapeDtypeStruct((rows, 2 * width), jnp.float32)
    return pl.pallas_call(
        functools.partial(outer_kernel, span),
        out_shape=(
            shape,
            shape,
            jax.ShapeDtypeStruct((chans, 4 * span), own.dtype),
            jax.ShapeDtypeStruct((rows, 4 * span), jnp.float32),
        ),
        in_specs=[pl.BlockSpec(memory_space=pltpu.SMEM)] + [IN_VMEM] * (3 + len(fars)),
        out_specs=(IN_VMEM,) * 4,
        scratch_shapes=pair_scratch(chans, rows, width, span),
        cost_estimate=pl.CostEstimate(flops=flops, bytes_accessed=1 << 20, transcendentals=0),
        compiler_params=pltpu.CompilerParams(vmem_limit_bytes=32 << 20),
    )(odd, weights, active, own, *fars)


def inner_kernel(span, weights, active, near, edges, squares, corr, energy, frames, partial):
    rows, width = corr.shape
    before, after = slice(2 * span, 3 * span), slice(span, 2 * span)
    signal = jnp.concatenate([edges[:, before], near[...], edges[:, after]], 1)
    sums = channel_squares(active[...], near[...])
    sums = jnp.concatenate([squares[:, before], sums, squares[:, after]], 1)
    energy[...] = line_sums(sums, span)[:, :width]
    corr[...] = correlate(weights, signal, frames, partial, rows, width)


def inner_call(weights, active, near, edges, squares, span):
    rows, chans = active.shape
    width = span + near.shape[1]
    flops = 2 * weights.shape[0] * weights.shape[1] * width
    shape = jax.ShapeDtypeStruct((rows, width), jnp.float32)
    return pl.pallas_call(
        functools.partial(inner_kernel, span),
        out_shape=(shape, shape),
        in_specs=[IN_VMEM] * 5,
        out_specs=(IN_VMEM,) * 2,
        scratch_shapes=pair_scratch(chans, rows, width, span),
        cost_estimate=pl.CostEstimate(flops=flops, bytes_accessed=1 << 20, transcendentals=0),
        compiler_params=pltpu.CompilerParams(vmem_limit_bytes=32 << 20),
    )(weights, active, near, edges, squares)


def middle_kernel(span, missing, weights, active, part, edges, squares, corr, energy, frames, partial):
    rows, width = corr.shape
    gap = jnp.zeros((part.shape[0], missing), part.dtype)
    before, after = slice(3 * span, 4 * span), slice(0, span)
    signal = jnp.concatenate([edges[:, before], part[...], gap, edges[:, after]], 1)
    sums = channel_squares(active[...], part[...])
    gap = jnp.zeros((rows, missing), jnp.float32)
    sums = jnp.concatenate([squares[:, before], sums, gap, squares[:, after]], 1)
    energy[...] = line_sums(sums, span)[:, :width]
    corr[...] = correlate(weights, signal, frames, partial, rows, width)


def middle_call(weights, active, part, edges, squares, missing, span):
    rows, chans = active.shape
    width = span + part.shape[1] + missing
    flops = 2 * weights.shape[0] * weights.shape[1] * width
    shape = jax.ShapeDtypeStruct((rows, width), jnp.float32)
    return pl.pallas_call(
        functools.partial(middle_kernel, span, missing),
        out_shape=(shape, shape),
        in_specs=[IN_VMEM] * 5,
        out_specs=(IN_VMEM,) * 2,
        scratch_shapes=pair_scratch(chans, rows, width, span),
        cost_estimate=pl.CostEstimate(flops=flops, bytes_accessed=1 << 20, transcendentals=0),
        compiler_params=pltpu.CompilerParams(vmem_limit_bytes=32 << 20),
    )(weights, active, part, edges, squares)


def late_kernel(span, ways, table, place, weights, active, part, outer_corr, outer_energy, inner_corr, inner_energy, middle_corr, middle_energy, *refs):
    outs, (corr_all, energy_all, frames, partial) = refs[:ways], refs[ways:]
    rows, total = corr_all.shape
    side, inner = outer_corr.shape[1] // 2, inner_corr.shape[1]
    start = total - span - part.shape[1]
    kept = start - 2 * side - inner
    sums = channel_squares(active[...], part[...])
    sums = line_sums(jnp.concatenate([jnp.zeros((rows, span), jnp.float32), sums], 1), span)
    alone = correlate_alone(weights, part[...], frames, partial, rows)
    for whole, outer, between, middle, added in (
        (energy_all, outer_energy, inner_energy, middle_energy, sums),
        (corr_all, outer_corr, inner_corr, middle_corr, alone),
    ):
        whole[:, :side] = outer[:, :side]
        whole[:, side : side + inner] = between[...]
        whole[:, side + inner : 2 * side + inner] = outer[:, side:]
        whole[:, start - kept : start] = middle[:, :kept]
        whole[:, start:] = middle[:, kept:] + added
    share(place, table, total // len(table), corr_all, energy_all, outs)


def late_call(place, table, weights, active, part, early, middle, span, ways):
    rows = active.shape[0]
    chans, width = part.shape
    total = sum(early[index].shape[1] for index in (0, 2)) + middle[0].shape[1]
    shape = jax.ShapeDtypeStruct((2 * rows, total // ways), jnp.float32)
    flops = 2 * weights.shape[0] * weights.shape[1] * width
    return pl.pallas_call(
        functools.partial(late_kernel, span, ways, table),
        out_shape=(shape,) * ways,
        in_specs=[pl.BlockSpec(memory_space=pltpu.SMEM)] + [IN_VMEM] * (3 + len(early) + len(middle)),
        out_specs=(IN_VMEM,) * ways,
        scratch_shapes=[pltpu.VMEM((rows, total), jnp.float32)] * 2
        + [
            pltpu.VMEM((FRAMES * chans, width + LANE), jnp.bfloat16),
            pltpu.VMEM((weights.shape[0], width + LANE), jnp.float32),
        ],
        cost_estimate=pl.CostEstimate(flops=flops, bytes_accessed=1 << 20, transcendentals=0),
        compiler_params=pltpu.CompilerParams(vmem_limit_bytes=32 << 20),
    )(place, weights, active, part, *early, *middle)


def share(place, table, tile, corr_all, energy_all, outs):
    rows, total = corr_all.shape
    ways = len(outs)
    count = total // tile // ways
    for shift in range(ways):
        group = lax.rem(place[0] + shift, ways) * count
        for item in range(count):
            position = group + item
            if table:
                position = jnp.int32(0)
                for home, row in enumerate(table):
                    for slot, value in enumerate(row):
                        chosen = (place[1] == home) & (group + item == slot)
                        position = jnp.where(chosen, value, position)
            start = pl.multiple_of(position * tile, LANE)
            columns = slice(item * tile, (item + 1) * tile)
            outs[shift][0:rows, columns] = corr_all[:, pl.ds(start, tile)]
            outs[shift][rows : 2 * rows, columns] = energy_all[:, pl.ds(start, tile)]


def line_sums(values, span):
    reach = 1
    while reach < span:
        ways = 4 if 4 * reach <= span else 2
        moved = [
            jnp.concatenate([values[:, by * reach :], values[:, : by * reach]], 1) for by in range(1, ways)
        ]
        values = sum(moved, values)
        reach *= ways
    return values


def pack_kernel(span, tile, pairs, place, *refs):
    corrs, squares = refs[:pairs], refs[pairs : 2 * pairs]
    outs, corr_all, energy_all = refs[2 * pairs : -2], refs[-2], refs[-1]
    corr = jnp.concatenate([ref[...] for ref in corrs], 1)
    corr_all[...] = jnp.concatenate([corr[:, tile:], corr[:, :tile]], 1)
    energy = line_sums(jnp.concatenate([ref[...] for ref in squares], 1), span)
    energy_all[...] = jnp.concatenate([energy[:, tile:], energy[:, :tile]], 1)
    share(place, None, tile, corr_all, energy_all, outs)


def pack_call(place, corrs, squares, span, ways):
    rows, width = corrs[0].shape
    pairs = len(corrs)
    total = pairs * width
    shape = jax.ShapeDtypeStruct((2 * rows, total // ways), jnp.float32)
    return pl.pallas_call(
        functools.partial(pack_kernel, span, width // 2, pairs),
        out_shape=(shape,) * ways,
        in_specs=[pl.BlockSpec(memory_space=pltpu.SMEM)] + [IN_VMEM] * (2 * pairs),
        out_specs=(IN_VMEM,) * ways,
        scratch_shapes=[pltpu.VMEM((rows, total), jnp.float32)] * 2,
        compiler_params=pltpu.CompilerParams(vmem_limit_bytes=16 << 20),
    )(place, *corrs, *squares)


def split_kernel(ways, count, place, *refs):
    ins, outs, held = refs[:count], refs[count:-1], refs[-1]
    total = ins[0][...]
    for ref in ins[1:]:
        total = total + ref[...]
    held[...] = total
    part = held.shape[1] // ways
    for shift in range(ways):
        start = pl.multiple_of(lax.rem(place[0] + shift, ways) * part, LANE)
        outs[shift][...] = held[:, pl.ds(start, part)]


def split_call(place, parts, ways):
    rows, width = parts[0].shape
    shape = jax.ShapeDtypeStruct((rows, width // ways), jnp.float32)
    return pl.pallas_call(
        functools.partial(split_kernel, ways, len(parts)),
        out_shape=(shape,) * ways,
        in_specs=[pl.BlockSpec(memory_space=pltpu.SMEM)] + [IN_VMEM] * len(parts),
        out_specs=(IN_VMEM,) * ways,
        scratch_shapes=[pltpu.VMEM((rows, width), jnp.float32)],
        compiler_params=pltpu.CompilerParams(vmem_limit_bytes=16 << 20),
    )(place, *parts)


def score_kernel(span, count, stats, *refs):
    ins, out = refs[:count], refs[count]
    total = ins[0][...]
    for ref in ins[1:]:
        total = total + ref[...]
    rows = out.shape[0]
    template_energy = stats[0:rows, 0:1]
    active_count = stats[rows:, 0:1]
    factor = jnp.sqrt(span * active_count)
    energy = total[rows:, :]
    out[...] = total[0:rows, :] * factor / jnp.sqrt(energy * template_energy + EPSILON)


def score_call(stats, parts, span):
    rows, width = parts[0].shape
    return pl.pallas_call(
        functools.partial(score_kernel, span, len(parts)),
        out_shape=jax.ShapeDtypeStruct((rows // 2, width), jnp.float32),
        in_specs=[IN_VMEM] * (1 + len(parts)),
        out_specs=IN_VMEM,
        compiler_params=pltpu.CompilerParams(vmem_limit_bytes=16 << 20),
    )(stats, *parts)


def exchange(parts, axis):
    return [parts[0]] + [shifted(part, axis, shift) for shift, part in enumerate(parts) if shift]


def paired(x, axis, bit):
    return lax.ppermute(x, axis, [(i, i ^ bit) for i in range(lax.axis_size(axis))])


def relays(circle, ways):
    return circle == ways == 4


def relayed_sums(traces, weights, active, place, table, span, ways):
    half = traces.shape[1] // 2
    fars = [paired(traces[:, :half], "tm", 2)]
    fars.append(paired(traces[:, half:], "tm", 2))
    near = paired(traces, "tm", 1)
    before = paired(fars[0], "tm", 1)
    part = paired(fars[1], "tm", 1)
    odd = (lax.axis_index("tm") % 2).astype(jnp.int32)[None]
    *outer, edges, squares = outer_call(odd, weights, active, traces, fars, span)
    early = (*outer, *inner_call(weights, active, near, edges, squares, span))
    middle = middle_call(weights, active, before, edges, squares, part.shape[1], span)
    return late_call(place, table, weights, active, part, early, middle, span, ways)


def routes(circle, chan_ways, sub_ways):
    held = circle // (chan_ways * sub_ways)
    table = []
    for place in range(circle):
        chan = place // held // sub_ways
        slots = [(s, c, h) for s in range(sub_ways) for c in range(chan_ways) for h in range(held)]
        tiles = sorted(range(circle), key=lambda t: -abs(t - place))
        ranked = sorted(range(circle), key=lambda k: (slots[k][1] != chan, -slots[k][0]))
        row = [0] * circle
        for slot, time_tile in zip(ranked, tiles):
            row[slot] = time_tile
        table.append(row)
    return table


def gathered_sums(traces, weights, active, place, table, span, ways):
    circle = lax.axis_size("tm")
    arrived = {0: traces}
    for hop in range(1, circle // 2 + 1):
        for near in dict.fromkeys((hop, circle - hop)):
            arrived[near] = shifted(traces, "tm", -near)
    corrs, squares = [], []
    for pair in range(circle // 2):
        first, second = arrived[(2 * pair - 1) % circle], arrived[2 * pair]
        head = arrived[(2 * pair + 1) % circle]
        corr, square = pair_call(weights, active, first, second, head, span)
        corrs.append(corr)
        squares.append(square)
    return pack_call(place, corrs, squares, span, ways)


def on_device(traces, templates, channel_mask):
    tile = traces.shape[1]
    rows, _, span = templates.shape
    circle = lax.axis_size("tm")
    chan_ways, sub_ways = lax.axis_size("chan"), lax.axis_size("sub")
    active = channel_mask.astype(jnp.bfloat16)
    masked = templates * active[:, :, None]
    weights = arrange(masked, span)
    wide = masked.astype(jnp.float32)
    template_energy = jnp.sum(wide * wide, axis=(1, 2))
    active_count = jnp.sum(channel_mask, axis=1).astype(jnp.float32)
    stats = jnp.broadcast_to(jnp.concatenate([template_energy, active_count])[:, None], (2 * rows, LANE))
    for axis in ("sub", "chan"):
        others = [shifted(stats, axis, by) for by in range(1, lax.axis_size(axis))]
        stats = sum(others, stats)
    place = jnp.stack([lax.axis_index("sub"), lax.axis_index("tm")]).astype(jnp.int32)
    chan_place = lax.axis_index("chan").astype(jnp.int32)[None]

    ways = chan_ways * sub_ways
    held = circle // ways
    relayed = relays(circle, ways)
    if relayed:
        table = routes(circle, chan_ways, sub_ways)
    else:
        table = [[(slot + place) % circle for slot in range(circle)] for place in range(circle)]
    sums = relayed_sums if relayed else gathered_sums
    spots = [[(time_tile + home) % circle for time_tile in row] for home, row in enumerate(table)]
    parts = sums(traces, weights, active, place, spots, span, sub_ways)
    parts = exchange(parts, "sub")
    parts = exchange(split_call(chan_place, parts, chan_ways), "chan")
    scores = score_call(stats, parts, span)

    received = []
    for piece in range(held):
        pairs = []
        for place in range(circle):
            for chan in range(chan_ways):
                for sub in range(sub_ways):
                    source = (place * chan_ways + chan) * sub_ways + sub
                    slot = (sub * chan_ways + chan) * held + piece
                    pairs.append((source, table[place][slot] * ways + place // held))
        block = scores[:, piece * tile : (piece + 1) * tile]
        received.append(lax.ppermute(block, ("tm", "chan", "sub"), pairs))
    if held == 1:
        return received[0]
    turn = (lax.axis_index("tm") - jnp.arange(held)) % held
    return jnp.stack(received)[turn].reshape(held * rows, tile)


def solution(mesh):
    placed = (
        P(("chan", "sub"), ("groups", "tm")),
        P("tm", ("chan", "sub"), None),
        P("tm", ("chan", "sub")),
    )
    return jax.shard_map(
        on_device,
        mesh=mesh,
        in_specs=placed,
        out_specs=P(("chan", "sub"), ("groups", "tm")),
        check_vma=False,
    )
```
